32 devices in a mesh: rep: 4 (over y, core), fsdp: 4 (over z), tp: 2 (over x).
Axes of the slice: x: 2, y: 2, z: 4, core: 2. Of those that a mesh axis runs over, the one named last changes fastest.
Arguments:
- tokens: bfloat16 [5632, 1024], P(('rep', 'fsdp')), may hold values from -6 to 6
- segment_ids: int32 [5632], P(('rep', 'fsdp')), may hold values from 0 to 11, as said below
- valid_keys: int32 [5632], P(('rep', 'fsdp')), may hold values 0 or 1
- norm_gain: bfloat16 [1, 2, 1024], P(None, None, 'fsdp'), may hold values from 0.25 to 1.75
- norm_bias: bfloat16 [1, 2, 1024], P(None, None, 'fsdp'), may hold values from -3 to 3
- qkv_weight: bfloat16 [1, 1024, 3, 1024], P(None, 'fsdp', None, 'tp')
- qv_bias: bfloat16 [1, 2, 16, 64], P(None, None, 'tp', 'fsdp'), may hold values from -3 to 3
- out_weight: bfloat16 [1, 1024, 1024], P(None, 'tp', 'fsdp'), may hold values from -1 to 1
- up_weight: bfloat16 [1, 1024, 4096], P(None, 'fsdp', 'tp'), may hold values from -0.1875 to 0.1875
- up_bias: bfloat16 [1, 64, 64], P(None, 'tp', 'fsdp'), may hold values from -3 to 3
- down_weight: bfloat16 [1, 4096, 1024], P(None, 'tp', 'fsdp'), may hold values from -0.09375 to 0.09375
- out_bias: bfloat16 [1, 2, 1024], P(None, None, 'fsdp'), may hold values from -2 to 2
- layer_scale: bfloat16 [1, 2, 1024], P(None, None, 'fsdp'), may hold values from 0.29882812 to 1
- cotangent: bfloat16 [5632, 1024], P(('rep', 'fsdp')), may hold values from -6 to 6
Outputs:
- block_out: bfloat16 [5632, 1024], P(('rep', 'fsdp'))
- tokens_grad: float32 [5632, 1024], P(('rep', 'fsdp'))
- norm_gain_grad: float32 [1, 2, 1024], P(None, None, 'fsdp')
- norm_bias_grad: float32 [1, 2, 1024], P(None, None, 'fsdp')
- qkv_weight_grad: float32 [1, 1024, 3, 1024], P(None, 'fsdp', None, 'tp')
- qv_bias_grad: float32 [1, 2, 16, 64], P(None, None, 'tp', 'fsdp')
- out_weight_grad: float32 [1, 1024, 1024], P(None, 'tp', 'fsdp')
- up_weight_grad: float32 [1, 1024, 4096], P(None, 'fsdp', 'tp')
- up_bias_grad: float32 [1, 64, 64], P(None, 'tp', 'fsdp')
- down_weight_grad: float32 [1, 4096, 1024], P(None, 'tp', 'fsdp')
- out_bias_grad: float32 [1, 2, 1024], P(None, None, 'fsdp')
- layer_scale_grad: float32 [1, 2, 1024], P(None, None, 'fsdp')
The draws below stay inside these ranges and needn't reach their ends.
Inputs may be any that keep to these rules, and one draw needn't show every extreme that they name: `segment_ids`: non-decreasing along the tokens; no segment crosses a block of 1408 tokens (one index of rep); each such block holds (1406) // 1370 images of exactly 1370 consecutive tokens, with a piece of 1 or more tokens before them and one after them, each piece a segment of its own.
All inputs are finite; a program needn't handle non-finite values. No bound on the sum of `valid_keys` on one device may be relied on, other than what follows from the above.
Results may differ from the reference program's by a relative error of at most 0.014.
Values may be sent and summed in bfloat16 or wider, within the bound.
No kernel may reach another device: no remote copies, remote signals or barrier semaphores. Data moves between devices by JAX's collectives and lax.ppermute only.
A program may use at most 128 MiB of HBM per device.

```python
import math
import jax
import jax.numpy as jnp
from jax import lax

D = 1024
H = 16
HD = 64
FF = 4096
L = 1
IMG_LEN = 1370
GROUP_TOK = 1408
TOK_DEV = 352
TOKENS = 5632
REACH = 3


def draw_segment_ids(key, part):
    group_count = TOKENS // GROUP_TOK
    full_images = (GROUP_TOK - 2) // IMG_LEN
    spare = GROUP_TOK - full_images * IMG_LEN
    starts = jax.random.randint(jax.random.fold_in(key, 11), (group_count,), 1, spare)
    positions = jnp.arange(GROUP_TOK, dtype=jnp.int32)
    relative = positions[None, :] - starts[:, None]
    inner = jnp.where(relative < 0, 0, jnp.where(relative >= full_images * IMG_LEN, full_images + 1, relative // IMG_LEN + 1))
    base = (jnp.arange(group_count, dtype=jnp.int32) * (full_images + 2))[:, None]
    return (inner + base).reshape(-1).astype(jnp.int32)


def draw_qkv_weight(key, part):
    base_key = jax.random.fold_in(jax.random.fold_in(key, 7), 0)
    scale = D ** (-0.5)
    values = jnp.clip(jax.random.normal(base_key, (L, D, 3, D), jnp.float32), -4.0, 4.0) * scale
    return values.astype(jnp.bfloat16)


def plant(result, own_key, least, high):
    dims = result.shape
    spot = [jax.random.randint(jax.random.fold_in(own_key, axis), (), 0, dims[axis]) for axis in range(len(dims))]
    result = result.at[tuple(spot)].set(least)
    longest = dims.index(max(dims))
    spot[longest] = (spot[longest] + 1) % dims[longest]
    return result.at[tuple(spot)].set(high)


def level_of(stream_key, dims, cuts, low, largest):
    level, own = 1.0, jax.random.fold_in(stream_key, 6)
    for dim, shards_of in cuts:
        steps = jnp.exp(jax.random.uniform(jax.random.fold_in(own, dim), (shards_of,), jnp.float32, low / len(cuts), largest / len(cuts)))
        level = level * jnp.repeat(steps, dims[dim] // shards_of).reshape([-1 if axis == dim else 1 for axis in range(len(dims))])
    return level


def scatter_about(rng, shape, deviation, limit, pieces=(), kind=jnp.bfloat16):
    values = deviation * jax.random.normal(rng, shape, jnp.float32)
    if pieces:
        values = values * level_of(rng, shape, pieces, -0.22, 0.18)
    return jnp.clip(values, -limit, limit).astype(kind)


def setup_inputs(seed: int = 0) -> dict:
    key_list = jax.random.split(jax.random.key(seed), 15)
    return {
        "tokens": scatter_about(key_list[0], (TOKENS, D), 1.0, 6.0, ((0, 16),)),
        "segment_ids": draw_segment_ids(jax.random.fold_in(key_list[14], 71), 0),
        "valid_keys": plant((jax.random.randint(key_list[2], (TOKENS,), 0, 8) < 7).astype(jnp.int32), jax.random.fold_in(key_list[2], 1), 0, 1),
        "norm_gain": jnp.clip(1.0 + 0.15 * jax.random.normal(key_list[3], (L, 2, D), jnp.float32), 0.25, 1.75).astype(jnp.bfloat16),
        "norm_bias": scatter_about(key_list[4], (L, 2, D), 0.5, 3.0, ((2, 4),)),
        "qkv_weight": draw_qkv_weight(jax.random.fold_in(key_list[14], 71), 0),
        "qv_bias": scatter_about(key_list[6], (L, 2, H, HD), 0.5, 3.0, ((2, 2), (3, 4))),
        "out_weight": scatter_about(key_list[7], (L, D, D), (D // 32) ** -0.5, 1.0, ((1, 2), (2, 4))),
        "up_weight": scatter_about(key_list[8], (L, D, FF), D ** -0.5, 0.1875, ((1, 4), (2, 2))),
        "up_bias": scatter_about(key_list[9], (L, FF // HD, HD), 0.5, 3.0, ((1, 2), (2, 4))),
        "down_weight": scatter_about(key_list[10], (L, FF, D), FF ** -0.5, 0.09375, ((1, 2), (2, 4))),
        "out_bias": scatter_about(key_list[11], (L, 2, D), 0.3, 2.0, ((2, 4),)),
        "layer_scale": jnp.clip(jnp.exp(math.log(1.0) - 1.2078867 * jax.random.uniform(key_list[12], (L, 2, D), jnp.float32) ** level_of(key_list[12], (L, 2, D), ((2, 4),), -0.2, 0.2)), 0.29882812, 1.0).astype(jnp.bfloat16),
        "cotangent": scatter_about(key_list[13], (TOKENS, D), 1.0, 6.0, ((0, 16),)),
    }


EPSILON = 1e-06
ROOT_HALF = 0.7071067811865476
INV_ROOT_TWO_PI = 0.3989422804014327
NEG_LARGE = -1e+30

def to_half(values):
    return lax.optimization_barrier(values.astype(jnp.bfloat16))

def norm_forward(values, gain, shift):
    centred = values - lax.optimization_barrier(jnp.mean(values, axis=-1, keepdims=True))
    inverse = lax.rsqrt(lax.optimization_barrier(jnp.mean(centred * centred, axis=-1, keepdims=True)) + EPSILON)
    normal_part = centred * inverse
    return (normal_part * gain + shift, normal_part, inverse)

def norm_backward(upstream, normal_part, inverse, gain):
    scaled = upstream * gain
    inner = scaled - lax.optimization_barrier(jnp.mean(scaled, axis=-1, keepdims=True)) - normal_part * lax.optimization_barrier(jnp.mean(scaled * normal_part, axis=-1, keepdims=True))
    return (inverse * inner, lax.optimization_barrier(jnp.sum(upstream * normal_part, axis=0)), lax.optimization_barrier(jnp.sum(upstream, axis=0)))

def gelu_value(pre):
    return 0.5 * pre * (1.0 + lax.erf(pre * ROOT_HALF))

def gelu_slope(pre):
    return 0.5 * (1.0 + lax.erf(pre * ROOT_HALF)) + pre * INV_ROOT_TWO_PI * jnp.exp(-0.5 * pre * pre)

def allowed_keys(query_seg, key_code, query_count):
    key_seg = key_code // 2
    key_live = key_code % 2
    positions = jnp.arange(key_code.shape[0], dtype=jnp.int32)
    diagonal = positions[None, :] == jnp.arange(query_count, dtype=jnp.int32)[:, None] + REACH * query_count
    return (query_seg[:, None] == key_seg[None, :]) & ((key_live[None, :] == 1) | diagonal)

def padded_inputs(keys, values, key_code):
    margin = REACH * TOK_DEV
    keys_pad = jnp.pad(keys, ((margin, margin), (0, 0), (0, 0)))
    values_pad = jnp.pad(values, ((margin, margin), (0, 0), (0, 0)))
    code_pad = jnp.pad(key_code, (margin, margin))
    return (keys_pad, values_pad, code_pad)

def attention_forward(query, keys, values, segment_ids, key_code):
    window = (2 * REACH + 1) * TOK_DEV
    keys_pad, values_pad, code_pad = padded_inputs(keys, values, key_code)
    score_scale = HD ** (-0.5)

    def block(block_index):
        start = block_index * TOK_DEV
        query_block = lax.dynamic_slice_in_dim(query, start, TOK_DEV, 0).astype(jnp.float32)
        key_block = lax.dynamic_slice_in_dim(keys_pad, start, window, 0).astype(jnp.float32)
        value_block = lax.dynamic_slice_in_dim(values_pad, start, window, 0).astype(jnp.float32)
        allowed = allowed_keys(lax.dynamic_slice_in_dim(segment_ids, start, TOK_DEV, 0), lax.dynamic_slice_in_dim(code_pad, start, window, 0), TOK_DEV)
        scores = jnp.einsum('qhd,khd->hqk', query_block, key_block) * score_scale
        scores = jnp.where(allowed[None], scores, NEG_LARGE)
        top = lax.optimization_barrier(jnp.max(scores, axis=2, keepdims=True))
        expo = jnp.where(allowed[None], jnp.exp(scores - top), 0.0)
        total = lax.optimization_barrier(jnp.sum(expo, axis=2, keepdims=True))
        weights = to_half(expo / total).astype(jnp.float32)
        mixed = jnp.einsum('hqk,khd->qhd', weights, value_block)
        return (to_half(mixed), (top + jnp.log(total))[:, :, 0])
    block_out, log_total = lax.map(block, jnp.arange(TOKENS // TOK_DEV, dtype=jnp.int32))
    return (block_out.reshape(TOKENS, H, HD), log_total)

def attention_backward(query, keys, values, mixed, d_mixed, log_total, segment_ids, key_code):
    margin = REACH * TOK_DEV
    window = (2 * REACH + 1) * TOK_DEV
    keys_pad, values_pad, code_pad = padded_inputs(keys, values, key_code)
    score_scale = HD ** (-0.5)

    def block(carry, block_index):
        start = block_index * TOK_DEV
        query_block = lax.dynamic_slice_in_dim(query, start, TOK_DEV, 0).astype(jnp.float32)
        out_block = lax.dynamic_slice_in_dim(mixed, start, TOK_DEV, 0).astype(jnp.float32)
        grad_block = lax.dynamic_slice_in_dim(d_mixed, start, TOK_DEV, 0).astype(jnp.float32)
        key_block = lax.dynamic_slice_in_dim(keys_pad, start, window, 0).astype(jnp.float32)
        value_block = lax.dynamic_slice_in_dim(values_pad, start, window, 0).astype(jnp.float32)
        allowed = allowed_keys(lax.dynamic_slice_in_dim(segment_ids, start, TOK_DEV, 0), lax.dynamic_slice_in_dim(code_pad, start, window, 0), TOK_DEV)
        scores = jnp.einsum('qhd,khd->hqk', query_block, key_block) * score_scale
        probs = jnp.where(allowed[None], jnp.exp(scores - log_total[block_index][:, :, None]), 0.0)
        d_value = jnp.einsum('hqk,qhd->khd', to_half(probs).astype(jnp.float32), grad_block)
        d_probs = jnp.einsum('qhd,khd->hqk', grad_block, value_block)
        inner = lax.optimization_barrier(jnp.sum(grad_block * out_block, axis=2))
        d_scores = to_half(probs * (d_probs - inner.T[:, :, None])).astype(jnp.float32)
        d_query = jnp.einsum('hqk,khd->qhd', d_scores, key_block) * score_scale
        d_key = jnp.einsum('hqk,qhd->khd', d_scores, query_block) * score_scale
        d_pair = jnp.stack([d_key, d_value], axis=1)
        current = lax.dynamic_slice_in_dim(carry, start, window, 0)
        carry = lax.dynamic_update_slice_in_dim(carry, current + d_pair, start, 0)
        return (carry, d_query)
    initial = jnp.zeros((TOKENS + 2 * margin, 2, H, HD), jnp.float32)
    carry, d_query = lax.scan(block, initial, jnp.arange(TOKENS // TOK_DEV, dtype=jnp.int32))
    d_pairs = carry[margin:margin + TOKENS]
    return (d_query.reshape(TOKENS, D), d_pairs[:, 0].reshape(TOKENS, D), d_pairs[:, 1].reshape(TOKENS, D))

def reference(tokens, segment_ids, valid_keys, norm_gain, norm_bias, qkv_weight, qv_bias, out_weight, up_weight, up_bias, down_weight, out_bias, layer_scale, cotangent):
    key_code = (segment_ids * 2 + valid_keys).astype(jnp.int32)
    resid = tokens.astype(jnp.float32)
    saved = []
    for layer_index in range(L):
        gains = norm_gain[layer_index].astype(jnp.float32)
        shifts = norm_bias[layer_index].astype(jnp.float32)
        biases = out_bias[layer_index].astype(jnp.float32)
        scales = layer_scale[layer_index].astype(jnp.float32)
        query_bias = qv_bias[layer_index].astype(jnp.float32).reshape(2, D)
        normed, part_one, inv_one = norm_forward(resid, gains[0], shifts[0])
        first_in = to_half(normed)
        project = jnp.dot(first_in, qkv_weight[layer_index].reshape(D, 3 * D), preferred_element_type=jnp.float32).reshape(TOKENS, 3, D)
        query = to_half(project[:, 0] + query_bias[0]).reshape(TOKENS, H, HD)
        keys = to_half(project[:, 1]).reshape(TOKENS, H, HD)
        values = to_half(project[:, 2] + query_bias[1]).reshape(TOKENS, H, HD)
        mixed, log_total = attention_forward(query, keys, values, segment_ids, key_code)
        mixed_flat = mixed.reshape(TOKENS, D)
        branch_one = jnp.dot(mixed_flat, out_weight[layer_index], preferred_element_type=jnp.float32) + biases[0]
        resid_one = resid + scales[0] * branch_one
        normed_two, part_two, inv_two = norm_forward(resid_one, gains[1], shifts[1])
        second_in = to_half(normed_two)
        hidden_pre = jnp.dot(second_in, up_weight[layer_index], preferred_element_type=jnp.float32) + up_bias[layer_index].astype(jnp.float32).reshape(FF)
        hidden = to_half(gelu_value(hidden_pre))
        branch_two = jnp.dot(hidden, down_weight[layer_index], preferred_element_type=jnp.float32) + biases[1]
        saved.append((part_one, inv_one, first_in, query, keys, values, mixed, log_total, mixed_flat, branch_one, part_two, inv_two, second_in, hidden_pre, hidden, branch_two))
        resid = resid_one + scales[1] * branch_two
    block_out = resid.astype(jnp.bfloat16)
    grads = [None] * L
    upstream = cotangent.astype(jnp.float32)
    for layer_index in reversed(range(L)):
        part_one, inv_one, first_in, query, keys, values, mixed, log_total, mixed_flat, branch_one, part_two, inv_two, second_in, hidden_pre, hidden, branch_two = saved[layer_index]
        gains = norm_gain[layer_index].astype(jnp.float32)
        scales = layer_scale[layer_index].astype(jnp.float32)
        scale_two = lax.optimization_barrier(jnp.sum(upstream * branch_two, axis=0))
        bias_two = lax.optimization_barrier(jnp.sum(upstream * scales[1], axis=0))
        branch_grad = to_half(upstream * scales[1])
        d_down = jnp.dot(hidden.T, branch_grad, preferred_element_type=jnp.float32)
        d_hidden = jnp.dot(branch_grad, down_weight[layer_index].T, preferred_element_type=jnp.float32) * gelu_slope(hidden_pre)
        d_up_bias = lax.optimization_barrier(jnp.sum(d_hidden, axis=0))
        d_hidden_half = to_half(d_hidden)
        d_up = jnp.dot(second_in.T, d_hidden_half, preferred_element_type=jnp.float32)
        d_second = jnp.dot(d_hidden_half, up_weight[layer_index].T, preferred_element_type=jnp.float32)
        d_norm_two, gain_two, shift_two = norm_backward(d_second, part_two, inv_two, gains[1])
        upstream_one = upstream + d_norm_two
        scale_one = lax.optimization_barrier(jnp.sum(upstream_one * branch_one, axis=0))
        bias_one = lax.optimization_barrier(jnp.sum(upstream_one * scales[0], axis=0))
        branch_grad_one = to_half(upstream_one * scales[0])
        d_out = jnp.dot(mixed_flat.T, branch_grad_one, preferred_element_type=jnp.float32)
        d_mixed = to_half(jnp.dot(branch_grad_one, out_weight[layer_index].T, preferred_element_type=jnp.float32))
        d_query, d_key, d_value = attention_backward(query, keys, values, mixed, d_mixed.reshape(TOKENS, H, HD), log_total, segment_ids, key_code)
        d_qv = jnp.stack([lax.optimization_barrier(jnp.sum(d_query, axis=0)), lax.optimization_barrier(jnp.sum(d_value, axis=0))]).reshape(2, H, HD)
        d_project = to_half(jnp.stack([d_query, d_key, d_value], axis=1).reshape(TOKENS, 3 * D))
        d_qkv = jnp.dot(first_in.T, d_project, preferred_element_type=jnp.float32).reshape(D, 3, D)
        d_first = jnp.dot(d_project, qkv_weight[layer_index].reshape(D, 3 * D).T, preferred_element_type=jnp.float32)
        d_norm_one, gain_one, shift_one = norm_backward(d_first, part_one, inv_one, gains[0])
        upstream = upstream_one + d_norm_one
        grads[layer_index] = (jnp.stack([gain_one, gain_two]), jnp.stack([shift_one, shift_two]), d_qkv, d_qv, d_out, d_up, d_up_bias.reshape(FF // HD, HD), d_down, jnp.stack([bias_one, bias_two]), jnp.stack([scale_one, scale_two]))
    stacked = [jnp.stack([grads[layer_index][member] for layer_index in range(L)]) for member in range(10)]
    return (block_out, upstream, stacked[0], stacked[1], stacked[2], stacked[3], stacked[4], stacked[5], stacked[6], stacked[7], stacked[8], stacked[9])
```

```python
import functools

import jax
import jax.numpy as jnp
from jax import lax
from jax.experimental import pallas as pl
from jax.experimental.pallas import tpu as pltpu
from jax.sharding import PartitionSpec as P

HD = 64
QB = 128
EPSILON = 1e-06
ROOT_HALF = 0.7071067811865476
INV_ROOT_TWO_PI = 0.3989422804014327
NEG_LARGE = -1e30
BF = jnp.bfloat16
F32 = jnp.float32


def norm_forward(values, gain, shift):
    centred = values - jnp.mean(values, axis=-1, keepdims=True)
    inverse = lax.rsqrt(jnp.mean(centred * centred, axis=-1, keepdims=True) + EPSILON)
    normal_part = centred * inverse
    return (normal_part * gain + shift, normal_part, inverse)


def norm_backward(upstream, normal_part, inverse, gain):
    scaled = upstream * gain
    inner = (
        scaled
        - jnp.mean(scaled, axis=-1, keepdims=True)
        - normal_part * jnp.mean(scaled * normal_part, axis=-1, keepdims=True)
    )
    return (inverse * inner, jnp.sum(upstream * normal_part, axis=0), jnp.sum(upstream, axis=0))


def gelu_value(pre):
    return 0.5 * pre * (1.0 + lax.erf(pre * ROOT_HALF))


def gelu_slope(pre):
    return 0.5 * (1.0 + lax.erf(pre * ROOT_HALF)) + pre * INV_ROOT_TWO_PI * jnp.exp(
        -0.5 * pre * pre
    )


def dot(a, b):
    return jnp.dot(a, b, preferred_element_type=F32)


def dot_nt(a, b):
    return lax.dot_general(a, b, (((1,), (1,)), ((), ())), preferred_element_type=F32)


def dot_tn(a, b):
    return lax.dot_general(a, b, (((0,), (0,)), ((), ())), preferred_element_type=F32)


def spread_heads(rows, heads):
    wide = rows.astype(F32)
    lane_head = lax.broadcasted_iota(jnp.int32, wide.shape, 1) // HD
    parts = [jnp.where(lane_head == h, wide, 0.0) for h in range(heads)]
    return jnp.concatenate(parts, axis=0).astype(BF)


def own_blocks(across, heads):
    return jnp.concatenate(
        [across[h * HD : (h + 1) * HD, h * QB : (h + 1) * QB] for h in range(heads)], axis=0
    )


def fill_bias(bias_ref, key_ref, query_row, off):
    bias_ref[...] = jnp.where(key_ref[...] == query_row, 0.0, NEG_LARGE)
    eye = lax.broadcasted_iota(jnp.int32, (QB, QB), 0) == lax.broadcasted_iota(
        jnp.int32, (QB, QB), 1
    )
    bias_ref[pl.ds(off, QB), :] = jnp.where(eye, 0.0, bias_ref[pl.ds(off, QB), :])


def forward_kernel(heads, x_ref, key_ref, seg_ref, o_ref, lse_ref, vt_ref, bias_ref):
    width = heads * HD
    total_rows = x_ref.shape[0]
    vt_ref[...] = x_ref[:, 2 * width : 3 * width].astype(F32).T.astype(BF)

    def step(i, carry):
        off = pl.multiple_of(i * QB, QB)
        query = spread_heads(x_ref[pl.ds(off, QB), 0:width] * (HD**-0.5), heads)
        fill_bias(bias_ref, key_ref, seg_ref[i], off)
        scores = dot_nt(x_ref[:, width : 2 * width], query)
        bias = bias_ref[...]
        scores = scores + jnp.concatenate([bias] * heads, axis=1)
        top = jnp.max(scores, axis=0, keepdims=True)
        expo = jnp.exp(scores - top)
        total = jnp.sum(expo, axis=0, keepdims=True)
        weights = (expo * (1.0 / total)).astype(BF)
        mixed = own_blocks(dot(vt_ref[...], weights), heads)
        o_ref[pl.ds(off, QB), :] = mixed.T.astype(BF)
        lse_ref[i] = top + jnp.log(total)
        return carry

    lax.fori_loop(0, total_rows // QB, step, 0)


def backward_kernel(
    heads,
    x_ref,
    o_ref,
    g_ref,
    lse_ref,
    key_ref,
    seg_ref,
    dx_ref,
    sums_ref,
    kt_ref,
    dk_ref,
    dv_ref,
    bias_ref,
):
    width = heads * HD
    total_rows = x_ref.shape[0]
    kt_ref[...] = x_ref[:, width : 2 * width].astype(F32).T.astype(BF)
    dk_ref[...] = jnp.zeros_like(dk_ref)
    dv_ref[...] = jnp.zeros_like(dv_ref)

    def step(i, query_sum):
        off = pl.multiple_of(i * QB, QB)
        query = spread_heads(x_ref[pl.ds(off, QB), 0:width] * (HD**-0.5), heads)
        g_rows = g_ref[pl.ds(off, QB), :]
        grad = spread_heads(g_rows, heads)
        product = (g_rows.astype(F32) * o_ref[pl.ds(off, QB), :].astype(F32)).T
        delta = jnp.concatenate(
            [
                jnp.sum(product[h * HD : (h + 1) * HD], axis=0, keepdims=True)
                for h in range(heads)
            ],
            axis=1,
        )
        fill_bias(bias_ref, key_ref, seg_ref[i], off)
        scores = dot_nt(x_ref[:, width : 2 * width], query)
        bias = bias_ref[...]
        probs = jnp.exp(scores + jnp.concatenate([bias] * heads, axis=1) - lse_ref[i])
        d_probs = dot_nt(x_ref[:, 2 * width : 3 * width], grad)
        dv_ref[...] += dot(probs.astype(BF), grad)
        d_scores = (probs * (d_probs - delta)).astype(BF)
        dk_ref[...] += dot(d_scores, query)
        d_query = own_blocks(dot(kt_ref[...], d_scores), heads).T * (HD**-0.5)
        dx_ref[pl.ds(off, QB), 0:width] = d_query.astype(BF)
        return query_sum + jnp.sum(d_query, axis=0, keepdims=True)

    query_sum = lax.fori_loop(0, total_rows // QB, step, jnp.zeros((1, width), F32))
    dx_ref[:, width : 2 * width] = dk_ref[...].astype(BF)
    dx_ref[:, 2 * width : 3 * width] = dv_ref[...].astype(BF)
    sums_ref[...] = jnp.concatenate(
        [query_sum, jnp.sum(dv_ref[...], axis=0, keepdims=True)], axis=0
    )


def attend_forward(x, key_codes, seg_rows, heads):
    rows = x.shape[0]
    width = heads * HD
    return pl.pallas_call(
        functools.partial(forward_kernel, heads),
        out_shape=(
            jax.ShapeDtypeStruct((rows, width), BF),
            jax.ShapeDtypeStruct((rows // QB, 1, heads * QB), F32),
        ),
        scratch_shapes=[pltpu.VMEM((width, rows), BF), pltpu.VMEM((rows, QB), F32)],
        cost_estimate=pl.CostEstimate(
            flops=4 * rows * rows * width,
            transcendentals=rows * rows * heads,
            bytes_accessed=rows * width * 8,
        ),
        name="attend_forward",
    )(x, key_codes, seg_rows)


def attend_backward(x, mixed, grad, lse, key_codes, seg_rows, heads):
    rows = x.shape[0]
    width = heads * HD
    return pl.pallas_call(
        functools.partial(backward_kernel, heads),
        out_shape=(
            jax.ShapeDtypeStruct((rows, 3 * width), BF),
            jax.ShapeDtypeStruct((2, width), F32),
        ),
        scratch_shapes=[
            pltpu.VMEM((width, rows), BF),
            pltpu.VMEM((rows, width), F32),
            pltpu.VMEM((rows, width), F32),
            pltpu.VMEM((rows, QB), F32),
        ],
        cost_estimate=pl.CostEstimate(
            flops=10 * rows * rows * width,
            transcendentals=rows * rows * heads,
            bytes_accessed=rows * width * 20,
        ),
        name="attend_backward",
    )(x, mixed, grad, lse, key_codes, seg_rows)


def after(value, *others):
    return lax.optimization_barrier((value, *others))[0]


def local(
    n,
    reps,
    tokens,
    segment_ids,
    valid_keys,
    norm_gain,
    norm_bias,
    qkv_weight,
    qv_bias,
    out_weight,
    up_weight,
    up_bias,
    down_weight,
    out_bias,
    layer_scale,
    cotangent,
):
    rows, width = tokens.shape
    ys = reps // 2
    local_heads = qv_bias.shape[2]
    hidden = up_weight.shape[2]
    heads = local_heads // n
    head_cols = heads * HD
    unit_cols = hidden // reps
    part = width // n
    z = lax.axis_index("fsdp")
    rep = lax.axis_index("rep")
    y, core = rep // 2, rep % 2

    def z_pull(x, s):
        return lax.ppermute(x, "fsdp", [((j + s) % n, j) for j in range(n)])

    def z_push(x, s):
        return z_pull(x, n - s)

    def y_pull(x, d):
        return lax.ppermute(
            x, "rep", [(((a + d) % ys) * 2 + c, a * 2 + c) for a in range(ys) for c in range(2)]
        )

    def y_push(x, d):
        return y_pull(x, ys - d)

    def core_swap(x):
        return lax.ppermute(x, "rep", [(r, r ^ 1) for r in range(reps)])

    def gather_z(x):
        return [x] + [z_pull(x, s) for s in range(1, n)]

    def gather_rep(x):
        near = [x] + [y_pull(x, d) for d in range(1, ys)]
        return near + [core_swap(v) for v in near]

    slot_rep = [((y + d) % ys) * 2 + core for d in range(ys)]
    slot_rep = slot_rep + [((y + d) % ys) * 2 + 1 - core for d in range(ys)]

    def in_rep_order(slots, axis):
        stacked = jnp.stack(slots)
        picks = []
        for a in range(reps):
            slot = (a // 2 - y) % ys + ys * ((a % 2) ^ core)
            picks.append(lax.dynamic_index_in_dim(stacked, slot, 0, keepdims=False))
        return jnp.concatenate(picks, axis=axis)

    def from_own(x, axis, block):
        return lax.dynamic_slice_in_dim(
            jnp.concatenate([x, x], axis=axis), z * block, x.shape[axis], axis
        )

    def to_plain(x, axis, block):
        return lax.dynamic_slice_in_dim(
            jnp.concatenate([x, x], axis=axis), ((n - z) % n) * block, x.shape[axis], axis
        )

    def sum_tp(x):
        mine = x
        return mine + lax.ppermute(mine, "tp", [(0, 1), (1, 0)])

    def exchange_heads(slots):
        stacked = jnp.stack(slots)
        blocks = [lax.dynamic_index_in_dim(stacked, z, 0, keepdims=False)]
        for s in range(1, n):
            out = lax.dynamic_index_in_dim(stacked, (z + n - s) % n, 0, keepdims=False)
            blocks.append(z_pull(out, s))
        return jnp.concatenate(blocks, axis=0)

    def return_heads(x):
        blocks = [x[s * rows : (s + 1) * rows] for s in range(n)]
        return [blocks[0]] + [z_pull(blocks[n - s], s) for s in range(1, n)]

    q_cols = local_heads * HD // reps
    piece_qkv = lax.dynamic_slice_in_dim(qkv_weight[0], rep * q_cols, q_cols, 2).reshape(
        part, 3 * q_cols
    )
    piece_out = lax.dynamic_slice_in_dim(out_weight[0], rep * q_cols, q_cols, 0)
    piece_up = lax.dynamic_slice_in_dim(up_weight[0], rep * unit_cols, unit_cols, 1)
    piece_down = lax.dynamic_slice_in_dim(down_weight[0], rep * unit_cols, unit_cols, 0)

    codes = (segment_ids * 2 + valid_keys).astype(F32).astype(BF)
    code_rows = -(-rows // part)
    codes = jnp.pad(codes, (0, code_rows * part - rows)).reshape(code_rows, part)
    features = jnp.concatenate([norm_gain[0], norm_bias[0], out_bias[0], layer_scale[0], codes])
    units = jnp.concatenate([qv_bias.reshape(2 * local_heads, -1), up_bias[0]])

    gathered_qkv = gather_z(piece_qkv)
    gathered_features = gather_z(features)
    gathered_units = gather_z(units)
    slots_qkv = gather_rep(jnp.concatenate(gathered_qkv, axis=0))
    w_qkv = jnp.concatenate(slots_qkv, axis=1)

    piece_out = after(piece_out, *gathered_qkv)
    piece_up = after(piece_up, *gathered_qkv)
    w_out = jnp.concatenate(gather_rep(jnp.concatenate(gather_z(piece_out), axis=1)), axis=0)
    w_up = jnp.concatenate(gather_rep(jnp.concatenate(gather_z(piece_up), axis=0)), axis=1)

    small = jnp.concatenate([f[:8] for f in gathered_features], axis=1).astype(F32)
    gains, shifts, biases, scales = small[0:2], small[2:4], small[4:6], small[6:8]
    all_codes = jnp.concatenate([f[8:].reshape(-1)[:rows] for f in gathered_features])
    all_codes = all_codes.astype(jnp.int32)
    group_seg = all_codes // 2
    key_codes = jnp.where(all_codes % 2 == 1, group_seg, -1)
    group_rows = all_codes.shape[0]
    key_codes = jnp.broadcast_to(key_codes[:, None], (group_rows, QB))
    seg_rows = group_seg.reshape(group_rows // QB, 1, QB)
    unit_lanes = units.shape[1]
    units_full = to_plain(jnp.concatenate(gathered_units, axis=1), 1, unit_lanes).astype(F32)
    qv_full = units_full[: 2 * local_heads].reshape(2, local_heads * HD)
    up_full = units_full[2 * local_heads :].reshape(-1)
    qv_slots = [lax.dynamic_slice_in_dim(qv_full, r * q_cols, q_cols, 1) for r in slot_rep]
    up_slots = jnp.concatenate(
        [lax.dynamic_slice_in_dim(up_full, r * unit_cols, unit_cols, 0) for r in slot_rep]
    )
    bias_qkv = jnp.concatenate(
        [jnp.concatenate([b[0], jnp.zeros((q_cols,), F32), b[1]]) for b in qv_slots]
    )

    resid = from_own(tokens, 1, part).astype(F32)
    upstream = from_own(cotangent, 1, part).astype(F32)

    normed, part_one, inv_one = norm_forward(resid, gains[0], shifts[0])
    first_in = normed.astype(BF)
    project = (dot(first_in, w_qkv) + bias_qkv).astype(BF)
    slot_cols = 3 * head_cols
    x_heads = exchange_heads([project[:, k * slot_cols : (k + 1) * slot_cols] for k in range(n)])
    piece_down = after(piece_down, x_heads)
    w_down = jnp.concatenate(gather_rep(jnp.concatenate(gather_z(piece_down), axis=1)), axis=0)
    mixed, lse = attend_forward(x_heads, key_codes, seg_rows, heads)
    mixed_slots = to_plain(jnp.stack(return_heads(mixed)), 0, 1)
    mixed_flat = jnp.concatenate([mixed_slots[k] for k in range(n)], axis=1)
    branch_one = sum_tp(dot(mixed_flat, w_out)) + biases[0]
    resid_one = resid + scales[0] * branch_one
    normed_two, part_two, inv_two = norm_forward(resid_one, gains[1], shifts[1])
    second_in = normed_two.astype(BF)
    hidden_pre = dot(second_in, w_up) + up_slots
    hidden_act = gelu_value(hidden_pre).astype(BF)
    branch_two = sum_tp(dot(hidden_act, w_down)) + biases[1]
    block_out = to_plain((resid_one + scales[1] * branch_two).astype(BF), 1, part)

    def reduce_grad(lead, tail, slot_axis, z_axis):
        total = lead + core_swap(tail)
        step = total.shape[slot_axis] // ys
        cuts = [lax.slice_in_dim(total, d * step, (d + 1) * step, axis=slot_axis) for d in range(ys)]
        mine = cuts[0]
        for d in range(1, ys):
            mine = mine + y_push(cuts[d].astype(BF), d).astype(F32)
        block = mine.shape[z_axis] // n
        blocks = [lax.slice_in_dim(mine, s * block, (s + 1) * block, axis=z_axis) for s in range(n)]
        result = blocks[0]
        for s in range(1, n):
            result = result + z_push(blocks[s], s)
        return gather_rep(result)

    scale_two = jnp.sum(upstream * branch_two, axis=0)
    bias_two = jnp.sum(upstream * scales[1], axis=0)
    branch_grad = (upstream * scales[1]).astype(BF)
    half = hidden // 2
    grad_down = reduce_grad(
        dot_tn(hidden_act[:, :half], branch_grad), dot_tn(hidden_act[:, half:], branch_grad), 0, 1
    )
    d_hidden = dot_nt(branch_grad, w_down) * gelu_slope(hidden_pre)
    d_up_bias = jnp.sum(d_hidden, axis=0)
    d_hidden_half = d_hidden.astype(BF)
    grad_up = reduce_grad(
        dot_tn(second_in, d_hidden_half[:, :half]), dot_tn(second_in, d_hidden_half[:, half:]), 1, 0
    )
    d_second = sum_tp(dot_nt(d_hidden_half, w_up))
    d_norm_two, gain_two, shift_two = norm_backward(d_second, part_two, inv_two, gains[1])
    upstream_one = upstream + d_norm_two
    scale_one = jnp.sum(upstream_one * branch_one, axis=0)
    bias_one = jnp.sum(upstream_one * scales[0], axis=0)
    branch_grad_one = (upstream_one * scales[0]).astype(BF)
    half = mixed_flat.shape[1] // 2
    grad_out = reduce_grad(
        dot_tn(mixed_flat[:, :half], branch_grad_one),
        dot_tn(mixed_flat[:, half:], branch_grad_one),
        0,
        1,
    )
    d_mixed = dot_nt(branch_grad_one, w_out).astype(BF)
    g_heads = exchange_heads([d_mixed[:, k * head_cols : (k + 1) * head_cols] for k in range(n)])
    dx_heads, head_sums = attend_backward(
        x_heads, mixed, g_heads, lse, key_codes, seg_rows, heads
    )
    dx_slots = to_plain(jnp.stack(return_heads(dx_heads)), 0, 1)
    d_project = jnp.concatenate([dx_slots[k] for k in range(n)], axis=1)
    half = d_project.shape[1] // 2
    grad_qkv = reduce_grad(
        dot_tn(first_in, d_project[:, :half]), dot_tn(first_in, d_project[:, half:]), 1, 0
    )
    d_first = sum_tp(dot_nt(d_project, w_qkv))
    d_norm_one, gain_one, shift_one = norm_backward(d_first, part_one, inv_one, gains[0])
    tokens_grad = to_plain(upstream_one + d_norm_one, 1, part)

    feature_grads = to_plain(
        jnp.stack(
            [gain_one, gain_two, shift_one, shift_two, bias_one, bias_two, scale_one, scale_two]
        ),
        1,
        part,
    )
    own_rep = lax.dynamic_index_in_dim(jnp.stack(slot_rep), z, 0, keepdims=False)
    qv_grads = lax.dynamic_update_slice_in_dim(
        jnp.zeros((2, local_heads * HD), F32), head_sums, own_rep * head_cols, 1
    )
    up_grads = in_rep_order(
        [d_up_bias[k * unit_cols : (k + 1) * unit_cols] for k in range(reps)], 0
    )
    packed = jnp.concatenate(
        [feature_grads.reshape(-1), qv_grads.reshape(-1), up_grads]
    ).reshape(-1, 128)

    def total_over(values, position, count):
        stacked = jnp.stack(values)
        turned = lax.dynamic_slice_in_dim(
            jnp.concatenate([stacked, stacked]), (count - position) % count, count, 0
        )
        return jnp.sum(turned, axis=0)

    packed = total_over([packed] + [z_pull(packed, s) for s in range(1, n)], z, n)
    packed = total_over([packed] + [y_pull(packed, d) for d in range(1, ys)], y, ys)
    packed = packed + core_swap(packed)
    packed = packed.reshape(-1)
    size_f, size_q = 8 * width, 2 * local_heads * HD
    feature_grads = lax.dynamic_slice_in_dim(
        packed[:size_f].reshape(4, 2, width), z * part, part, 2
    )
    qv_grads = lax.dynamic_slice_in_dim(
        packed[size_f : size_f + size_q].reshape(2, local_heads, HD), z * unit_lanes, unit_lanes, 2
    )
    up_grads = lax.dynamic_slice_in_dim(
        packed[size_f + size_q :].reshape(-1, HD), z * unit_lanes, unit_lanes, 1
    )

    d_qkv = in_rep_order([g.reshape(part, 3, q_cols) for g in grad_qkv], 2)
    return (
        block_out,
        tokens_grad,
        feature_grads[0][None],
        feature_grads[1][None],
        d_qkv[None],
        qv_grads[None],
        in_rep_order(grad_out, 0)[None],
        in_rep_order(grad_up, 1)[None],
        up_grads[None],
        in_rep_order(grad_down, 0)[None],
        feature_grads[2][None],
        feature_grads[3][None],
    )


def solution(mesh):
    n, reps, tp = mesh.shape["fsdp"], mesh.shape["rep"], mesh.shape["tp"]
    assert n == reps and tp == 2
    by_token = P(("rep", "fsdp"), None)
    by_feature = P(None, None, "fsdp")
    by_row = P(None, "fsdp", "tp")
    by_column = P(None, "tp", "fsdp")
    placed = (
        by_token,
        P(("rep", "fsdp")),
        P(("rep", "fsdp")),
        by_feature,
        by_feature,
        P(None, "fsdp", None, "tp"),
        P(None, None, "tp", "fsdp"),
        by_column,
        by_row,
        by_column,
        by_column,
        by_feature,
        by_feature,
        by_token,
    )
    return jax.shard_map(
        functools.partial(local, n, reps),
        mesh=mesh,
        in_specs=placed,
        out_specs=(
            by_token,
            by_token,
            by_feature,
            by_feature,
            P(None, "fsdp", None, "tp"),
            P(None, None, "tp", "fsdp"),
            by_column,
            by_row,
            by_column,
            by_column,
            by_feature,
            by_feature,
        ),
        check_vma=False,
    )
```

```python
import functools

import jax
import jax.numpy as jnp
from jax import lax
from jax.experimental import pallas as pl
from jax.experimental.pallas import tpu as pltpu
from jax.sharding import PartitionSpec as P


HD = 64
QB = 128
EPSILON = 1e-06
ROOT_HALF = 0.7071067811865476
INV_ROOT_TWO_PI = 0.3989422804014327
NEG_LARGE = -1e30
BF = jnp.bfloat16
F32 = jnp.float32


def norm_forward(values, gain, shift):
    centred = values - jnp.mean(values, axis=-1, keepdims=True)
    inverse = lax.rsqrt(jnp.mean(centred * centred, axis=-1, keepdims=True) + EPSILON)
    normal_part = centred * inverse
    return (normal_part * gain + shift, normal_part, inverse)


def norm_backward(upstream, normal_part, inverse, gain):
    scaled = upstream * gain
    inner = (
        scaled
        - jnp.mean(scaled, axis=-1, keepdims=True)
        - normal_part * jnp.mean(scaled * normal_part, axis=-1, keepdims=True)
    )
    return (inverse * inner, jnp.sum(upstream * normal_part, axis=0), jnp.sum(upstream, axis=0))


def gelu_value(pre):
    return 0.5 * pre * (1.0 + lax.erf(pre * ROOT_HALF))


def gelu_slope(pre):
    return 0.5 * (1.0 + lax.erf(pre * ROOT_HALF)) + pre * INV_ROOT_TWO_PI * jnp.exp(
        -0.5 * pre * pre
    )


def dot(a, b):
    return jnp.dot(a, b, preferred_element_type=F32)


def dot_nt(a, b):
    return lax.dot_general(a, b, (((1,), (1,)), ((), ())), preferred_element_type=F32)


def dot_tn(a, b):
    return lax.dot_general(a, b, (((0,), (0,)), ((), ())), preferred_element_type=F32)


def spread_heads(rows, heads):
    wide = rows.astype(F32)
    lane_head = lax.broadcasted_iota(jnp.int32, wide.shape, 1) // HD
    parts = [jnp.where(lane_head == h, wide, 0.0) for h in range(heads)]
    return jnp.concatenate(parts, axis=0).astype(BF)


def own_blocks(across, heads):
    return jnp.concatenate(
        [across[h * HD : (h + 1) * HD, h * QB : (h + 1) * QB] for h in range(heads)], axis=0
    )


def fill_bias(bias_ref, key_ref, query_row, off):
    bias_ref[...] = jnp.where(key_ref[...] == query_row, 0.0, NEG_LARGE)
    eye = lax.broadcasted_iota(jnp.int32, (QB, QB), 0) == lax.broadcasted_iota(
        jnp.int32, (QB, QB), 1
    )
    bias_ref[pl.ds(off, QB), :] = jnp.where(eye, 0.0, bias_ref[pl.ds(off, QB), :])


def forward_kernel(heads, x_ref, key_ref, seg_ref, o_ref, lse_ref, vt_ref, bias_ref):
    width = heads * HD
    total_rows = x_ref.shape[0]
    vt_ref[...] = x_ref[:, 2 * width : 3 * width].astype(F32).T.astype(BF)

    def step(i, carry):
        off = pl.multiple_of(i * QB, QB)
        query = spread_heads(x_ref[pl.ds(off, QB), 0:width] * (HD**-0.5), heads)
        fill_bias(bias_ref, key_ref, seg_ref[i], off)
        scores = dot_nt(x_ref[:, width : 2 * width], query)
        bias = bias_ref[...]
        scores = scores + jnp.concatenate([bias] * heads, axis=1)
        top = jnp.max(scores, axis=0, keepdims=True)
        expo = jnp.exp(scores - top)
        total = jnp.sum(expo, axis=0, keepdims=True)
        weights = (expo * (1.0 / total)).astype(BF)
        mixed = own_blocks(dot(vt_ref[...], weights), heads)
        o_ref[pl.ds(off, QB), :] = mixed.T.astype(BF)
        lse_ref[i] = top + jnp.log(total)
        return carry

    lax.fori_loop(0, total_rows // QB, step, 0)


def backward_kernel(
    heads,
    x_ref,
    o_ref,
    g_ref,
    lse_ref,
    key_ref,
    seg_ref,
    dx_ref,
    sums_ref,
    kt_ref,
    dk_ref,
    dv_ref,
    bias_ref,
):
    width = heads * HD
    total_rows = x_ref.shape[0]
    kt_ref[...] = x_ref[:, width : 2 * width].astype(F32).T.astype(BF)
    dk_ref[...] = jnp.zeros_like(dk_ref)
    dv_ref[...] = jnp.zeros_like(dv_ref)

    def step(i, query_sum):
        off = pl.multiple_of(i * QB, QB)
        query = spread_heads(x_ref[pl.ds(off, QB), 0:width] * (HD**-0.5), heads)
        g_rows = g_ref[pl.ds(off, QB), :]
        grad = spread_heads(g_rows, heads)
        product = (g_rows.astype(F32) * o_ref[pl.ds(off, QB), :].astype(F32)).T
        delta = jnp.concatenate(
            [
                jnp.sum(product[h * HD : (h + 1) * HD], axis=0, keepdims=True)
                for h in range(heads)
            ],
            axis=1,
        )
        fill_bias(bias_ref, key_ref, seg_ref[i], off)
        scores = dot_nt(x_ref[:, width : 2 * width], query)
        bias = bias_ref[...]
        probs = jnp.exp(scores + jnp.concatenate([bias] * heads, axis=1) - lse_ref[i])
        d_probs = dot_nt(x_ref[:, 2 * width : 3 * width], grad)
        dv_ref[...] += dot(probs.astype(BF), grad)
        d_scores = (probs * (d_probs - delta)).astype(BF)
        dk_ref[...] += dot(d_scores, query)
        d_query = own_blocks(dot(kt_ref[...], d_scores), heads).T * (HD**-0.5)
        dx_ref[pl.ds(off, QB), 0:width] = d_query.astype(BF)
        return query_sum + jnp.sum(d_query, axis=0, keepdims=True)

    query_sum = lax.fori_loop(0, total_rows // QB, step, jnp.zeros((1, width), F32))
    dx_ref[:, width : 2 * width] = dk_ref[...].astype(BF)
    dx_ref[:, 2 * width : 3 * width] = dv_ref[...].astype(BF)
    sums_ref[...] = jnp.concatenate(
        [query_sum, jnp.sum(dv_ref[...], axis=0, keepdims=True)], axis=0
    )


def attend_forward(x, key_codes, seg_rows, heads):
    rows = x.shape[0]
    width = heads * HD
    return pl.pallas_call(
        functools.partial(forward_kernel, heads),
        out_shape=(
            jax.ShapeDtypeStruct((rows, width), BF),
            jax.ShapeDtypeStruct((rows // QB, 1, heads * QB), F32),
        ),
        scratch_shapes=[pltpu.VMEM((width, rows), BF), pltpu.VMEM((rows, QB), F32)],
        cost_estimate=pl.CostEstimate(
            flops=4 * rows * rows * width,
            transcendentals=rows * rows * heads,
            bytes_accessed=rows * width * 8,
        ),
        name="attend_forward",
    )(x, key_codes, seg_rows)


def attend_backward(x, mixed, grad, lse, key_codes, seg_rows, heads):
    rows = x.shape[0]
    width = heads * HD
    return pl.pallas_call(
        functools.partial(backward_kernel, heads),
        out_shape=(
            jax.ShapeDtypeStruct((rows, 3 * width), BF),
            jax.ShapeDtypeStruct((2, width), F32),
        ),
        scratch_shapes=[
            pltpu.VMEM((width, rows), BF),
            pltpu.VMEM((rows, width), F32),
            pltpu.VMEM((rows, width), F32),
            pltpu.VMEM((rows, QB), F32),
        ],
        cost_estimate=pl.CostEstimate(
            flops=10 * rows * rows * width,
            transcendentals=rows * rows * heads,
            bytes_accessed=rows * width * 20,
        ),
        name="attend_backward",
    )(x, mixed, grad, lse, key_codes, seg_rows)


def after(value, *others):
    return lax.optimization_barrier((value, *others))[0]


def local(
    n,
    reps,
    tokens,
    segment_ids,
    valid_keys,
    norm_gain,
    norm_bias,
    qkv_weight,
    qv_bias,
    out_weight,
    up_weight,
    up_bias,
    down_weight,
    out_bias,
    layer_scale,
    cotangent,
):
    rows, width = tokens.shape
    ys = reps // 2
    local_heads = qv_bias.shape[2]
    hidden = up_weight.shape[2]
    heads = local_heads // n
    head_cols = heads * HD
    unit_cols = hidden // reps
    part = width // n
    z = lax.axis_index("fsdp")
    rep = lax.axis_index("rep")
    y, core = rep // 2, rep % 2
    first_tp = lax.axis_index("tp") == 0

    def z_pull(x, s):
        return lax.ppermute(x, "fsdp", [((j + s) % n, j) for j in range(n)])

    def z_push(x, s):
        return z_pull(x, n - s)

    def y_pull(x, d):
        return lax.ppermute(
            x, "rep", [(((a + d) % ys) * 2 + c, a * 2 + c) for a in range(ys) for c in range(2)]
        )

    def y_push(x, d):
        return y_pull(x, ys - d)

    def core_swap(x):
        return lax.ppermute(x, "rep", [(r, r ^ 1) for r in range(reps)])

    def gather_z(x):
        return [x] + [z_pull(x, s) for s in range(1, n)]

    def gather_rep(x):
        near = [x] + [y_pull(x, d) for d in range(1, ys)]
        return near + [core_swap(v) for v in near]

    slot_rep = [((y + d) % ys) * 2 + core for d in range(ys)]
    slot_rep = slot_rep + [((y + d) % ys) * 2 + 1 - core for d in range(ys)]

    def in_rep_order(slots, axis):
        stacked = jnp.stack(slots)
        picks = []
        for a in range(reps):
            slot = (a // 2 - y) % ys + ys * ((a % 2) ^ core)
            picks.append(lax.dynamic_index_in_dim(stacked, slot, 0, keepdims=False))
        return jnp.concatenate(picks, axis=axis)

    def from_own(x, axis, block):
        return lax.dynamic_slice_in_dim(
            jnp.concatenate([x, x], axis=axis), z * block, x.shape[axis], axis
        )

    def to_plain(x, axis, block):
        return lax.dynamic_slice_in_dim(
            jnp.concatenate([x, x], axis=axis), ((n - z) % n) * block, x.shape[axis], axis
        )

    def tp_swap(x):
        return lax.ppermute(x, "tp", [(0, 1), (1, 0)])

    def both_tp(x, other):
        return jnp.where(first_tp, x, other), jnp.where(first_tp, other, x)

    def exchange_heads(slots):
        stacked = jnp.stack(slots)
        outs = [
            lax.dynamic_index_in_dim(stacked, (z + n - s) % n, 0, keepdims=False)
            for s in range(n)
        ]
        blocks = [outs[0]] + [z_pull(outs[s], s) for s in range(1, n)]
        return jnp.concatenate(blocks, axis=0)

    def return_heads(x):
        blocks = [x[s * rows : (s + 1) * rows] for s in range(n)]
        return [blocks[0]] + [z_pull(blocks[n - s], s) for s in range(1, n)]

    q_cols = local_heads * HD // reps
    piece_qkv = lax.dynamic_slice_in_dim(qkv_weight[0], rep * q_cols, q_cols, 2).reshape(
        part, 3 * q_cols
    )
    gathered_qkv = gather_z(piece_qkv)

    codes = (segment_ids * 2 + valid_keys).astype(F32).astype(BF)
    code_rows = -(-rows // part)
    codes = jnp.pad(codes, (0, code_rows * part - rows)).reshape(code_rows, part)
    units = jnp.concatenate([qv_bias.reshape(2 * local_heads, -1), up_bias[0]])
    unit_shape = units.shape
    features = jnp.concatenate(
        [norm_gain[0], norm_bias[0], out_bias[0], layer_scale[0], codes, units.reshape(-1, part)]
    )
    gathered_features = gather_z(after(features, piece_qkv))

    piece_up = jnp.concatenate(
        [
            lax.dynamic_slice_in_dim(up_weight[0], rep * unit_cols, unit_cols, 1),
            lax.dynamic_slice_in_dim(out_weight[0], rep * q_cols, q_cols, 0).T,
        ],
        axis=1,
    )
    piece_down = lax.dynamic_slice_in_dim(down_weight[0], rep * unit_cols, unit_cols, 0)
    slots_qkv = gather_rep(jnp.concatenate(gathered_qkv, axis=0))
    gathered_up = gather_z(piece_up)

    small = jnp.concatenate([f[:8] for f in gathered_features], axis=1).astype(F32)
    gains, shifts, biases, scales = small[0:2], small[2:4], small[4:6], small[6:8]
    all_codes = jnp.concatenate(
        [f[8 : 8 + code_rows].reshape(-1)[:rows] for f in gathered_features]
    )
    all_codes = all_codes.astype(jnp.int32)
    group_seg = all_codes // 2
    key_codes = jnp.where(all_codes % 2 == 1, group_seg, -1)
    group_rows = all_codes.shape[0]
    key_codes = jnp.broadcast_to(key_codes[:, None], (group_rows, QB))
    seg_rows = group_seg.reshape(group_rows // QB, 1, QB)
    unit_lanes = unit_shape[1]
    gathered_units = [f[8 + code_rows :].reshape(unit_shape) for f in gathered_features]
    units_full = to_plain(jnp.concatenate(gathered_units, axis=1), 1, unit_lanes).astype(F32)
    qv_full = units_full[: 2 * local_heads].reshape(2, local_heads * HD)
    up_full = units_full[2 * local_heads :].reshape(-1)
    qv_slots = [lax.dynamic_slice_in_dim(qv_full, r * q_cols, q_cols, 1) for r in slot_rep]
    up_slots = jnp.concatenate(
        [lax.dynamic_slice_in_dim(up_full, r * unit_cols, unit_cols, 0) for r in slot_rep]
    )
    bias_qkv = [jnp.concatenate([b[0], jnp.zeros((q_cols,), F32), b[1]]) for b in qv_slots]

    resid = from_own(tokens, 1, part).astype(F32)
    upstream = from_own(cotangent, 1, part).astype(F32)

    normed, part_one, inv_one = norm_forward(resid, gains[0], shifts[0])
    first_in = normed.astype(BF)
    project = [(dot(first_in, w) + b).astype(BF) for w, b in zip(slots_qkv, bias_qkv)]
    x_heads = exchange_heads(project)
    quarter_up = jnp.concatenate(gathered_up, axis=0)
    quarter_out = quarter_up[:, unit_cols:]
    out_halves = both_tp(quarter_out, tp_swap(quarter_out))
    slots_up = gather_rep(jnp.concatenate([quarter_up[:, :unit_cols], *out_halves], axis=1))
    gathered_down = gather_z(piece_down)
    mixed, lse = attend_forward(x_heads, key_codes, seg_rows, heads)
    mixed_back = return_heads(mixed)
    slots_down = gather_rep(jnp.concatenate(gathered_down, axis=1))
    mixed_slots = to_plain(jnp.stack(mixed_back), 0, 1)
    mixed_flat = jnp.concatenate([mixed_slots[k] for k in range(n)], axis=1)
    mixed_halves = both_tp(mixed_flat, tp_swap(mixed_flat))
    mixed_full = jnp.concatenate(
        [m[:, k * q_cols : (k + 1) * q_cols] for k in range(reps) for m in mixed_halves],
        axis=1,
    )
    w_out_full = jnp.concatenate([w[:, unit_cols:] for w in slots_up], axis=1)
    w_out = jnp.concatenate(
        [
            jnp.where(first_tp, w[:, unit_cols : unit_cols + q_cols], w[:, unit_cols + q_cols :])
            for w in slots_up
        ],
        axis=1,
    )
    w_up = jnp.concatenate([w[:, :unit_cols] for w in slots_up], axis=1)
    branch_one = dot_nt(mixed_full, w_out_full) + biases[0]
    resid_one = resid + scales[0] * branch_one
    normed_two, part_two, inv_two = norm_forward(resid_one, gains[1], shifts[1])
    second_in = normed_two.astype(BF)
    w_down = jnp.concatenate(slots_down, axis=0)
    hidden_pre = dot(second_in, w_up) + up_slots
    hidden_act = gelu_value(hidden_pre).astype(BF)

    def sum_rep(lead, tail, slot_axis, sent=BF):
        total = lead + core_swap(tail)
        step = total.shape[slot_axis] // ys
        cuts = [lax.slice_in_dim(total, d * step, (d + 1) * step, axis=slot_axis) for d in range(ys)]
        mine = cuts[0]
        for d in range(1, ys):
            moved = y_push(cuts[d].astype(sent), d)
            mine = mine + moved.astype(F32)
        return mine

    def scatter_z(mine, z_axis, sent=F32):
        block = mine.shape[z_axis] // n
        blocks = [lax.slice_in_dim(mine, s * block, (s + 1) * block, axis=z_axis) for s in range(n)]
        result = blocks[0]
        for s in range(1, n):
            moved = z_push(blocks[s].astype(sent), s)
            result = result + moved.astype(F32)
        return gather_rep(result)

    branch_grad = (upstream * scales[1]).astype(BF)
    d_hidden = dot_nt(branch_grad, w_down) * gelu_slope(hidden_pre)
    d_hidden_half = d_hidden.astype(BF)
    partial_second = dot_nt(d_hidden_half, w_up)
    d_second = partial_second + tp_swap(partial_second)

    half = hidden // 2
    down_far = dot_tn(hidden_act[:, half:], branch_grad)
    up_far = dot_tn(second_in, d_hidden_half[:, half:])
    down_near = dot_tn(hidden_act[:, :half], branch_grad)
    up_near = dot_tn(second_in, d_hidden_half[:, :half])
    own_down = sum_rep(down_near, down_far, 0, F32)
    own_up = sum_rep(up_near, up_far, 1, F32)

    partial_two = dot(after(hidden_act, partial_second), w_down)
    other_two = tp_swap(partial_two)
    d_up_bias = jnp.sum(d_hidden, axis=0)

    d_norm_two = norm_backward(d_second, part_two, inv_two, gains[1])[0]
    upstream_one = upstream + d_norm_two
    branch_grad_one = (upstream_one * scales[0]).astype(BF)
    d_mixed = dot(branch_grad_one, w_out).astype(BF)
    g_heads = exchange_heads([d_mixed[:, k * head_cols : (k + 1) * head_cols] for k in range(n)])
    half = mixed_flat.shape[1] // 2
    out_far = dot_tn(mixed_flat[:, half:], branch_grad_one)
    out_near = dot_tn(mixed_flat[:, :half], branch_grad_one)
    own_out = sum_rep(out_near, out_far, 0)
    grad_down = scatter_z(own_down, 1, BF)
    dx_heads, head_sums = attend_backward(x_heads, mixed, g_heads, lse, key_codes, seg_rows, heads)
    dx_back = return_heads(dx_heads)

    late = lax.optimization_barrier(
        (
            upstream,
            upstream_one,
            branch_one,
            resid_one,
            partial_two,
            other_two,
            d_second,
            part_two,
            dx_heads,
        )
    )
    late_up, late_up_one, late_one, late_resid, late_two, late_other, late_second, late_part = late[:8]
    branch_two = late_two + late_other + biases[1]
    block_out = to_plain((late_resid + scales[1] * branch_two).astype(BF), 1, part)
    scale_two = jnp.sum(late_up * branch_two, axis=0)
    bias_two = jnp.sum(late_up, axis=0) * scales[1]
    scale_one = jnp.sum(late_up_one * late_one, axis=0)
    bias_one = jnp.sum(late_up_one, axis=0) * scales[0]
    gain_two = jnp.sum(late_second * late_part, axis=0)
    shift_two = jnp.sum(late_second, axis=0)

    grad_up = scatter_z(own_up, 0, BF)
    grad_out = scatter_z(own_out, 1)
    dx_slots = to_plain(jnp.stack(dx_back), 0, 1)
    d_project = jnp.concatenate([dx_slots[k] for k in range(n)], axis=1)
    half = d_project.shape[1] // 2
    qkv_far = dot_tn(first_in, d_project[:, half:])
    qkv_near = dot_tn(first_in, d_project[:, :half])
    grad_qkv = scatter_z(sum_rep(qkv_near, qkv_far, 1), 0)
    w_qkv = jnp.concatenate(slots_qkv, axis=1)
    partial_first = dot_nt(d_project, w_qkv)
    d_first = partial_first + tp_swap(partial_first)
    d_norm_one, gain_one, shift_one = norm_backward(d_first, part_one, inv_one, gains[0])
    tokens_grad = to_plain(upstream_one + d_norm_one, 1, part)

    feature_grads = to_plain(
        jnp.stack(
            [gain_one, gain_two, shift_one, shift_two, bias_one, bias_two, scale_one, scale_two]
        ),
        1,
        part,
    )
    own_rep = lax.dynamic_index_in_dim(jnp.stack(slot_rep), z, 0, keepdims=False)
    qv_grads = lax.dynamic_update_slice_in_dim(
        jnp.zeros((2, local_heads * HD), F32), head_sums, own_rep * head_cols, 1
    )
    up_grads = in_rep_order(
        [d_up_bias[k * unit_cols : (k + 1) * unit_cols] for k in range(reps)], 0
    )
    packed = jnp.concatenate(
        [feature_grads.reshape(-1), qv_grads.reshape(-1), up_grads]
    ).reshape(-1, 128)

    def total_over(values, position, count):
        stacked = jnp.stack(values)
        turned = lax.dynamic_slice_in_dim(
            jnp.concatenate([stacked, stacked]), (count - position) % count, count, 0
        )
        return jnp.sum(turned, axis=0)

    packed = total_over([packed] + [z_pull(packed, s) for s in range(1, n)], z, n)
    packed = total_over([packed] + [y_pull(packed, d) for d in range(1, ys)], y, ys)
    packed = packed + core_swap(packed)
    packed = packed.reshape(-1)
    size_f, size_q = 8 * width, 2 * local_heads * HD
    feature_grads = lax.dynamic_slice_in_dim(
        packed[:size_f].reshape(4, 2, width), z * part, part, 2
    )
    qv_grads = lax.dynamic_slice_in_dim(
        packed[size_f : size_f + size_q].reshape(2, local_heads, HD), z * unit_lanes, unit_lanes, 2
    )
    up_grads = lax.dynamic_slice_in_dim(
        packed[size_f + size_q :].reshape(-1, HD), z * unit_lanes, unit_lanes, 1
    )

    d_qkv = in_rep_order([g.reshape(part, 3, q_cols) for g in grad_qkv], 2)
    return (
        block_out,
        tokens_grad,
        feature_grads[0][None],
        feature_grads[1][None],
        d_qkv[None],
        qv_grads[None],
        in_rep_order(grad_out, 0)[None],
        in_rep_order(grad_up, 1)[None],
        up_grads[None],
        in_rep_order(grad_down, 0)[None],
        feature_grads[2][None],
        feature_grads[3][None],
    )


def solution(mesh):
    n, reps, tp = mesh.shape["fsdp"], mesh.shape["rep"], mesh.shape["tp"]
    assert n == reps and tp == 2
    by_token = P(("rep", "fsdp"), None)
    by_feature = P(None, None, "fsdp")
    by_row = P(None, "fsdp", "tp")
    by_column = P(None, "tp", "fsdp")
    placed = (
        by_token,
        P(("rep", "fsdp")),
        P(("rep", "fsdp")),
        by_feature,
        by_feature,
        P(None, "fsdp", None, "tp"),
        P(None, None, "tp", "fsdp"),
        by_column,
        by_row,
        by_column,
        by_column,
        by_feature,
        by_feature,
        by_token,
    )
    return jax.shard_map(
        functools.partial(local, n, reps),
        mesh=mesh,
        in_specs=placed,
        out_specs=(
            by_token,
            by_token,
            by_feature,
            by_feature,
            P(None, "fsdp", None, "tp"),
            P(None, None, "tp", "fsdp"),
            by_column,
            by_row,
            by_column,
            by_column,
            by_feature,
            by_feature,
        ),
        check_vma=False,
    )
```

```python
import functools

import jax
import jax.numpy as jnp
from jax import lax
from jax.experimental import pallas as pl
from jax.experimental.pallas import tpu as pltpu
from jax.sharding import PartitionSpec as P


HD = 64
QB = 128
EPSILON = 1e-06
ROOT_HALF = 0.7071067811865476
INV_ROOT_TWO_PI = 0.3989422804014327
NEG_LARGE = -1e30
BF = jnp.bfloat16
F32 = jnp.float32


def norm_forward(values, gain, shift):
    centred = values - jnp.mean(values, axis=-1, keepdims=True)
    inverse = lax.rsqrt(jnp.mean(centred * centred, axis=-1, keepdims=True) + EPSILON)
    normal_part = centred * inverse
    return (normal_part * gain + shift, normal_part, inverse)


def norm_backward(upstream, normal_part, inverse, gain):
    scaled = upstream * gain
    inner = (
        scaled
        - jnp.mean(scaled, axis=-1, keepdims=True)
        - normal_part * jnp.mean(scaled * normal_part, axis=-1, keepdims=True)
    )
    return (inverse * inner, jnp.sum(upstream * normal_part, axis=0), jnp.sum(upstream, axis=0))


def gelu_value(pre):
    return 0.5 * pre * (1.0 + lax.erf(pre * ROOT_HALF))


def gelu_slope(pre):
    return 0.5 * (1.0 + lax.erf(pre * ROOT_HALF)) + pre * INV_ROOT_TWO_PI * jnp.exp(
        -0.5 * pre * pre
    )


def dot(a, b):
    return jnp.dot(a, b, preferred_element_type=F32)


def dot_nt(a, b):
    return lax.dot_general(a, b, (((1,), (1,)), ((), ())), preferred_element_type=F32)


def dot_tn(a, b):
    return lax.dot_general(a, b, (((0,), (0,)), ((), ())), preferred_element_type=F32)


def spread_heads(rows, heads):
    wide = rows.astype(F32)
    lane_head = lax.broadcasted_iota(jnp.int32, wide.shape, 1) // HD
    parts = [jnp.where(lane_head == h, wide, 0.0) for h in range(heads)]
    return jnp.concatenate(parts, axis=0).astype(BF)


def own_blocks(across, heads):
    return jnp.concatenate(
        [across[h * HD : (h + 1) * HD, h * QB : (h + 1) * QB] for h in range(heads)], axis=0
    )


def fill_bias(bias_ref, key_ref, query_row, off):
    bias_ref[...] = jnp.where(key_ref[...] == query_row, 0.0, NEG_LARGE)
    eye = lax.broadcasted_iota(jnp.int32, (QB, QB), 0) == lax.broadcasted_iota(
        jnp.int32, (QB, QB), 1
    )
    bias_ref[pl.ds(off, QB), :] = jnp.where(eye, 0.0, bias_ref[pl.ds(off, QB), :])


def forward_kernel(heads, x_ref, key_ref, seg_ref, o_ref, lse_ref, vt_ref, bias_ref):
    width = heads * HD
    total_rows = x_ref.shape[0]
    vt_ref[...] = x_ref[:, 2 * width : 3 * width].astype(F32).T.astype(BF)

    def step(i, carry):
        off = pl.multiple_of(i * QB, QB)
        query = spread_heads(x_ref[pl.ds(off, QB), 0:width] * (HD**-0.5), heads)
        fill_bias(bias_ref, key_ref, seg_ref[i], off)
        scores = dot_nt(x_ref[:, width : 2 * width], query)
        bias = bias_ref[...]
        scores = scores + jnp.concatenate([bias] * heads, axis=1)
        top = jnp.max(scores, axis=0, keepdims=True)
        expo = jnp.exp(scores - top)
        total = jnp.sum(expo, axis=0, keepdims=True)
        weights = (expo * (1.0 / total)).astype(BF)
        mixed = own_blocks(dot(vt_ref[...], weights), heads)
        o_ref[pl.ds(off, QB), :] = mixed.T.astype(BF)
        lse_ref[i] = top + jnp.log(total)
        return carry

    lax.fori_loop(0, total_rows // QB, step, 0)


def backward_kernel(
    heads,
    x_ref,
    o_ref,
    g_ref,
    lse_ref,
    key_ref,
    seg_ref,
    dx_ref,
    sums_ref,
    kt_ref,
    dk_ref,
    dv_ref,
    bias_ref,
):
    width = heads * HD
    total_rows = x_ref.shape[0]
    kt_ref[...] = x_ref[:, width : 2 * width].astype(F32).T.astype(BF)
    dk_ref[...] = jnp.zeros_like(dk_ref)
    dv_ref[...] = jnp.zeros_like(dv_ref)

    def step(i, query_sum):
        off = pl.multiple_of(i * QB, QB)
        query = spread_heads(x_ref[pl.ds(off, QB), 0:width] * (HD**-0.5), heads)
        g_rows = g_ref[pl.ds(off, QB), :]
        grad = spread_heads(g_rows, heads)
        product = (g_rows.astype(F32) * o_ref[pl.ds(off, QB), :].astype(F32)).T
        delta = jnp.concatenate(
            [
                jnp.sum(product[h * HD : (h + 1) * HD], axis=0, keepdims=True)
                for h in range(heads)
            ],
            axis=1,
        )
        fill_bias(bias_ref, key_ref, seg_ref[i], off)
        scores = dot_nt(x_ref[:, width : 2 * width], query)
        bias = bias_ref[...]
        probs = jnp.exp(scores + jnp.concatenate([bias] * heads, axis=1) - lse_ref[i])
        d_probs = dot_nt(x_ref[:, 2 * width : 3 * width], grad)
        dv_ref[...] += dot(probs.astype(BF), grad)
        d_scores = (probs * (d_probs - delta)).astype(BF)
        dk_ref[...] += dot(d_scores, query)
        d_query = own_blocks(dot(kt_ref[...], d_scores), heads).T * (HD**-0.5)
        dx_ref[pl.ds(off, QB), 0:width] = d_query.astype(BF)
        return query_sum + jnp.sum(d_query, axis=0, keepdims=True)

    query_sum = lax.fori_loop(0, total_rows // QB, step, jnp.zeros((1, width), F32))
    dx_ref[:, width : 2 * width] = dk_ref[...].astype(BF)
    dx_ref[:, 2 * width : 3 * width] = dv_ref[...].astype(BF)
    sums_ref[...] = jnp.concatenate(
        [query_sum, jnp.sum(dv_ref[...], axis=0, keepdims=True)], axis=0
    )


def attend_forward(x, key_codes, seg_rows, heads):
    rows = x.shape[0]
    width = heads * HD
    return pl.pallas_call(
        functools.partial(forward_kernel, heads),
        out_shape=(
            jax.ShapeDtypeStruct((rows, width), BF),
            jax.ShapeDtypeStruct((rows // QB, 1, heads * QB), F32),
        ),
        scratch_shapes=[pltpu.VMEM((width, rows), BF), pltpu.VMEM((rows, QB), F32)],
        cost_estimate=pl.CostEstimate(
            flops=4 * rows * rows * width,
            transcendentals=rows * rows * heads,
            bytes_accessed=rows * width * 8,
        ),
        name="attend_forward",
    )(x, key_codes, seg_rows)


def attend_backward(x, mixed, grad, lse, key_codes, seg_rows, heads):
    rows = x.shape[0]
    width = heads * HD
    return pl.pallas_call(
        functools.partial(backward_kernel, heads),
        out_shape=(
            jax.ShapeDtypeStruct((rows, 3 * width), BF),
            jax.ShapeDtypeStruct((2, width), F32),
        ),
        scratch_shapes=[
            pltpu.VMEM((width, rows), BF),
            pltpu.VMEM((rows, width), F32),
            pltpu.VMEM((rows, width), F32),
            pltpu.VMEM((rows, QB), F32),
        ],
        cost_estimate=pl.CostEstimate(
            flops=10 * rows * rows * width,
            transcendentals=rows * rows * heads,
            bytes_accessed=rows * width * 20,
        ),
        name="attend_backward",
    )(x, mixed, grad, lse, key_codes, seg_rows)


def after(value, *others):
    return lax.optimization_barrier((value, *others))[0]


def local(
    n,
    reps,
    tokens,
    segment_ids,
    valid_keys,
    norm_gain,
    norm_bias,
    qkv_weight,
    qv_bias,
    out_weight,
    up_weight,
    up_bias,
    down_weight,
    out_bias,
    layer_scale,
    cotangent,
):
    rows, width = tokens.shape
    ys = reps // 2
    local_heads = qv_bias.shape[2]
    hidden = up_weight.shape[2]
    heads = local_heads // n
    head_cols = heads * HD
    unit_cols = hidden // reps
    part = width // n
    z = lax.axis_index("fsdp")
    rep = lax.axis_index("rep")
    y, core = rep // 2, rep % 2
    first_tp = lax.axis_index("tp") == 0

    def z_pull(x, s):
        return lax.ppermute(x, "fsdp", [((j + s) % n, j) for j in range(n)])

    def z_push(x, s):
        return z_pull(x, n - s)

    def y_pull(x, d):
        return lax.ppermute(
            x, "rep", [(((a + d) % ys) * 2 + c, a * 2 + c) for a in range(ys) for c in range(2)]
        )

    def y_push(x, d):
        return y_pull(x, ys - d)

    def core_swap(x):
        return lax.ppermute(x, "rep", [(r, r ^ 1) for r in range(reps)])

    def gather_z(x):
        return [x] + [z_pull(x, s) for s in range(1, n)]

    def gather_rep(x):
        near = [x] + [y_pull(x, d) for d in range(1, ys)]
        return near + [core_swap(v) for v in near]

    slot_rep = [((y + d) % ys) * 2 + core for d in range(ys)]
    slot_rep = slot_rep + [((y + d) % ys) * 2 + 1 - core for d in range(ys)]

    def in_rep_order(slots, axis):
        stacked = jnp.stack(slots)
        picks = []
        for a in range(reps):
            slot = (a // 2 - y) % ys + ys * ((a % 2) ^ core)
            picks.append(lax.dynamic_index_in_dim(stacked, slot, 0, keepdims=False))
        return jnp.concatenate(picks, axis=axis)

    def from_own(x, axis, block):
        return lax.dynamic_slice_in_dim(
            jnp.concatenate([x, x], axis=axis), z * block, x.shape[axis], axis
        )

    def to_plain(x, axis, block):
        return lax.dynamic_slice_in_dim(
            jnp.concatenate([x, x], axis=axis), ((n - z) % n) * block, x.shape[axis], axis
        )

    def tp_swap(x):
        return lax.ppermute(x, "tp", [(0, 1), (1, 0)])

    def both_tp(x, other):
        return jnp.where(first_tp, x, other), jnp.where(first_tp, other, x)

    def exchange_heads(slots):
        stacked = jnp.stack(slots)
        outs = [
            lax.dynamic_index_in_dim(stacked, (z + n - s) % n, 0, keepdims=False)
            for s in range(n)
        ]
        blocks = [outs[0]] + [z_pull(outs[s], s) for s in range(1, n)]
        return jnp.concatenate(blocks, axis=0)

    def return_heads(x):
        blocks = [x[s * rows : (s + 1) * rows] for s in range(n)]
        return [blocks[0]] + [z_pull(blocks[n - s], s) for s in range(1, n)]

    q_cols = local_heads * HD // reps
    piece_qkv = lax.dynamic_slice_in_dim(qkv_weight[0], rep * q_cols, q_cols, 2).reshape(
        part, 3 * q_cols
    )
    gathered_qkv = gather_z(piece_qkv)

    codes = (segment_ids * 2 + valid_keys).astype(F32).astype(BF)
    code_rows = -(-rows // part)
    codes = jnp.pad(codes, (0, code_rows * part - rows)).reshape(code_rows, part)
    units = jnp.concatenate([qv_bias.reshape(2 * local_heads, -1), up_bias[0]])
    unit_shape = units.shape
    features = jnp.concatenate(
        [norm_gain[0], norm_bias[0], out_bias[0], layer_scale[0], codes, units.reshape(-1, part)]
    )
    gathered_features = gather_z(after(features, piece_qkv))

    piece_up = jnp.concatenate(
        [
            lax.dynamic_slice_in_dim(up_weight[0], rep * unit_cols, unit_cols, 1),
            lax.dynamic_slice_in_dim(out_weight[0], rep * q_cols, q_cols, 0).T,
        ],
        axis=1,
    )
    piece_down = lax.dynamic_slice_in_dim(down_weight[0], rep * unit_cols, unit_cols, 0)
    slots_qkv = gather_rep(jnp.concatenate(gathered_qkv, axis=0))
    gathered_up = gather_z(after(piece_up, *gathered_qkv))

    small = jnp.concatenate([f[:8] for f in gathered_features], axis=1).astype(F32)
    gains, shifts, biases, scales = small[0:2], small[2:4], small[4:6], small[6:8]
    all_codes = jnp.concatenate(
        [f[8 : 8 + code_rows].reshape(-1)[:rows] for f in gathered_features]
    )
    all_codes = all_codes.astype(jnp.int32)
    group_seg = all_codes // 2
    key_codes = jnp.where(all_codes % 2 == 1, group_seg, -1)
    group_rows = all_codes.shape[0]
    key_codes = jnp.broadcast_to(key_codes[:, None], (group_rows, QB))
    seg_rows = group_seg.reshape(group_rows // QB, 1, QB)
    unit_lanes = unit_shape[1]
    gathered_units = [f[8 + code_rows :].reshape(unit_shape) for f in gathered_features]
    units_full = to_plain(jnp.concatenate(gathered_units, axis=1), 1, unit_lanes).astype(F32)
    qv_full = units_full[: 2 * local_heads].reshape(2, local_heads * HD)
    up_full = units_full[2 * local_heads :].reshape(-1)
    qv_slots = [lax.dynamic_slice_in_dim(qv_full, r * q_cols, q_cols, 1) for r in slot_rep]
    up_slots = jnp.concatenate(
        [lax.dynamic_slice_in_dim(up_full, r * unit_cols, unit_cols, 0) for r in slot_rep]
    )
    bias_qkv = [jnp.concatenate([b[0], jnp.zeros((q_cols,), F32), b[1]]) for b in qv_slots]

    resid = from_own(tokens, 1, part).astype(F32)
    upstream = from_own(cotangent, 1, part).astype(F32)

    normed, part_one, inv_one = norm_forward(resid, gains[0], shifts[0])
    first_in = normed.astype(BF)
    project = [(dot(first_in, w) + b).astype(BF) for w, b in zip(slots_qkv, bias_qkv)]
    x_heads = exchange_heads(project)
    quarter_up = jnp.concatenate(gathered_up, axis=0)
    quarter_out = quarter_up[:, unit_cols:]
    out_halves = both_tp(quarter_out, tp_swap(quarter_out))
    slots_up = gather_rep(jnp.concatenate([quarter_up[:, :unit_cols], *out_halves], axis=1))
    gathered_down = gather_z(after(piece_down, x_heads))
    mixed, lse = attend_forward(x_heads, key_codes, seg_rows, heads)
    mixed_back = return_heads(mixed)
    slots_down = gather_rep(jnp.concatenate(gathered_down, axis=1))
    mixed_slots = to_plain(jnp.stack(mixed_back), 0, 1)
    mixed_flat = jnp.concatenate([mixed_slots[k] for k in range(n)], axis=1)
    mixed_halves = both_tp(mixed_flat, tp_swap(mixed_flat))
    mixed_full = jnp.concatenate(
        [m[:, k * q_cols : (k + 1) * q_cols] for k in range(reps) for m in mixed_halves],
        axis=1,
    )
    w_out_full = jnp.concatenate([w[:, unit_cols:] for w in slots_up], axis=1)
    w_out = jnp.concatenate(
        [
            jnp.where(first_tp, w[:, unit_cols : unit_cols + q_cols], w[:, unit_cols + q_cols :])
            for w in slots_up
        ],
        axis=1,
    )
    w_up = jnp.concatenate([w[:, :unit_cols] for w in slots_up], axis=1)
    branch_one = dot_nt(mixed_full, w_out_full) + biases[0]
    resid_one = resid + scales[0] * branch_one
    normed_two, part_two, inv_two = norm_forward(resid_one, gains[1], shifts[1])
    second_in = normed_two.astype(BF)
    hidden_pre = dot(second_in, w_up) + up_slots
    hidden_act = gelu_value(hidden_pre).astype(BF)

    def sum_rep(lead, tail, slot_axis, sent=BF):
        total = lead + core_swap(tail)
        step = total.shape[slot_axis] // ys
        cuts = [lax.slice_in_dim(total, d * step, (d + 1) * step, axis=slot_axis) for d in range(ys)]
        mine = cuts[0]
        for d in range(1, ys):
            moved = y_push(cuts[d].astype(sent), d)
            mine = mine + moved.astype(F32)
        return mine

    def scatter_z(mine, z_axis, sent=F32):
        block = mine.shape[z_axis] // n
        wire = mine.astype(sent)
        result = lax.slice_in_dim(mine, 0, block, axis=z_axis)
        for s in range(1, n):
            cut = lax.slice_in_dim(wire, s * block, (s + 1) * block, axis=z_axis)
            moved = z_push(cut, s)
            result = result + moved.astype(F32)
        return gather_rep(result)

    branch_grad = (upstream * scales[1]).astype(BF)
    d_hidden = jnp.concatenate(
        [
            dot_nt(branch_grad, w)
            * gelu_slope(hidden_pre[:, k * unit_cols : (k + 1) * unit_cols])
            for k, w in enumerate(slots_down)
        ],
        axis=1,
    )
    d_hidden_half = d_hidden.astype(BF)
    partial_second = dot_nt(d_hidden_half, w_up)
    d_second = partial_second + tp_swap(partial_second)

    half = hidden // 2
    down_far = dot_tn(hidden_act[:, half:], branch_grad)
    up_far = dot_tn(second_in, d_hidden_half[:, half:])
    down_near = dot_tn(hidden_act[:, :half], branch_grad)
    up_near = dot_tn(second_in, d_hidden_half[:, :half])
    own_down = sum_rep(down_near, down_far, 0, F32)
    own_up = sum_rep(up_near, up_far, 1, F32)

    late_act = after(hidden_act, partial_second)
    partial_two = functools.reduce(
        jnp.add,
        [
            dot(late_act[:, k * unit_cols : (k + 1) * unit_cols], w)
            for k, w in enumerate(slots_down)
        ],
    )
    other_two = tp_swap(partial_two)
    d_norm_two = norm_backward(d_second, part_two, inv_two, gains[1])[0]
    upstream_one = upstream + d_norm_two
    branch_grad_one = (upstream_one * scales[0]).astype(BF)
    d_mixed = dot(branch_grad_one, w_out).astype(BF)
    g_heads = exchange_heads([d_mixed[:, k * head_cols : (k + 1) * head_cols] for k in range(n)])
    half = mixed_flat.shape[1] // 2
    out_far = dot_tn(mixed_flat[:, half:], branch_grad_one)
    out_near = dot_tn(mixed_flat[:, :half], branch_grad_one)
    own_out = sum_rep(out_near, out_far, 0)
    grad_down = scatter_z(own_down, 1, BF)
    dx_heads, head_sums = attend_backward(x_heads, mixed, g_heads, lse, key_codes, seg_rows, heads)
    dx_back = return_heads(dx_heads)

    late = lax.optimization_barrier(
        (
            upstream,
            upstream_one,
            branch_one,
            resid_one,
            partial_two,
            other_two,
            d_second,
            part_two,
            d_hidden,
            dx_heads,
        )
    )
    late_up, late_up_one, late_one, late_resid, late_two, late_other, late_second, late_part = late[:8]
    late_hidden = late[8]
    branch_two = late_two + late_other + biases[1]
    block_out = to_plain((late_resid + scales[1] * branch_two).astype(BF), 1, part)
    scale_two = jnp.sum(late_up * branch_two, axis=0)
    bias_two = jnp.sum(late_up, axis=0) * scales[1]
    scale_one = jnp.sum(late_up_one * late_one, axis=0)
    bias_one = jnp.sum(late_up_one, axis=0) * scales[0]
    gain_two = jnp.sum(late_second * late_part, axis=0)
    shift_two = jnp.sum(late_second, axis=0)
    d_up_bias = jnp.sum(late_hidden, axis=0)

    grad_up = scatter_z(own_up, 0, BF)
    grad_out = scatter_z(own_out, 1)
    dx_slots = to_plain(jnp.stack(dx_back), 0, 1)
    d_project = jnp.concatenate([dx_slots[k] for k in range(n)], axis=1)
    half = d_project.shape[1] // 2
    qkv_far = dot_tn(first_in, d_project[:, half:])
    qkv_near = dot_tn(first_in, d_project[:, :half])
    grad_qkv = scatter_z(sum_rep(qkv_near, qkv_far, 1), 0)
    w_qkv = jnp.concatenate(slots_qkv, axis=1)
    partial_first = dot_nt(d_project, w_qkv)
    d_first = partial_first + tp_swap(partial_first)
    d_norm_one, gain_one, shift_one = norm_backward(d_first, part_one, inv_one, gains[0])
    tokens_grad = to_plain(upstream_one + d_norm_one, 1, part)

    feature_grads = to_plain(
        jnp.stack(
            [gain_one, gain_two, shift_one, shift_two, bias_one, bias_two, scale_one, scale_two]
        ),
        1,
        part,
    )
    own_rep = lax.dynamic_index_in_dim(jnp.stack(slot_rep), z, 0, keepdims=False)
    qv_grads = lax.dynamic_update_slice_in_dim(
        jnp.zeros((2, local_heads * HD), F32), head_sums, own_rep * head_cols, 1
    )
    up_grads = in_rep_order(
        [d_up_bias[k * unit_cols : (k + 1) * unit_cols] for k in range(reps)], 0
    )
    packed = jnp.concatenate(
        [feature_grads.reshape(-1), qv_grads.reshape(-1), up_grads]
    ).reshape(-1, 128)

    def total_over(values, position, count):
        stacked = jnp.stack(values)
        turned = lax.dynamic_slice_in_dim(
            jnp.concatenate([stacked, stacked]), (count - position) % count, count, 0
        )
        return jnp.sum(turned, axis=0)

    packed = total_over([packed] + [z_pull(packed, s) for s in range(1, n)], z, n)
    packed = total_over([packed] + [y_pull(packed, d) for d in range(1, ys)], y, ys)
    packed = packed + core_swap(packed)
    packed = packed.reshape(-1)
    size_f, size_q = 8 * width, 2 * local_heads * HD
    feature_grads = lax.dynamic_slice_in_dim(
        packed[:size_f].reshape(4, 2, width), z * part, part, 2
    )
    qv_grads = lax.dynamic_slice_in_dim(
        packed[size_f : size_f + size_q].reshape(2, local_heads, HD), z * unit_lanes, unit_lanes, 2
    )
    up_grads = lax.dynamic_slice_in_dim(
        packed[size_f + size_q :].reshape(-1, HD), z * unit_lanes, unit_lanes, 1
    )

    d_qkv = in_rep_order([g.reshape(part, 3, q_cols) for g in grad_qkv], 2)
    return (
        block_out,
        tokens_grad,
        feature_grads[0][None],
        feature_grads[1][None],
        d_qkv[None],
        qv_grads[None],
        in_rep_order(grad_out, 0)[None],
        in_rep_order(grad_up, 1)[None],
        up_grads[None],
        in_rep_order(grad_down, 0)[None],
        feature_grads[2][None],
        feature_grads[3][None],
    )


def solution(mesh):
    n, reps, tp = mesh.shape["fsdp"], mesh.shape["rep"], mesh.shape["tp"]
    assert n == reps and tp == 2
    by_token = P(("rep", "fsdp"), None)
    by_feature = P(None, None, "fsdp")
    by_row = P(None, "fsdp", "tp")
    by_column = P(None, "tp", "fsdp")
    placed = (
        by_token,
        P(("rep", "fsdp")),
        P(("rep", "fsdp")),
        by_feature,
        by_feature,
        P(None, "fsdp", None, "tp"),
        P(None, None, "tp", "fsdp"),
        by_column,
        by_row,
        by_column,
        by_column,
        by_feature,
        by_feature,
        by_token,
    )
    return jax.shard_map(
        functools.partial(local, n, reps),
        mesh=mesh,
        in_specs=placed,
        out_specs=(
            by_token,
            by_token,
            by_feature,
            by_feature,
            P(None, "fsdp", None, "tp"),
            P(None, None, "tp", "fsdp"),
            by_column,
            by_row,
            by_column,
            by_column,
            by_feature,
            by_feature,
        ),
        check_vma=False,
    )
```

```python
import functools

import jax
import jax.numpy as jnp
from jax import lax
from jax.experimental import pallas as pl
from jax.experimental.pallas import tpu as pltpu
from jax.sharding import PartitionSpec as P


HD = 64
QB = 128
EPSILON = 1e-06
ROOT_HALF = 0.7071067811865476
INV_ROOT_TWO_PI = 0.3989422804014327
NEG_LARGE = -1e30
BF = jnp.bfloat16
F32 = jnp.float32


def norm_forward(values, gain, shift):
    centred = values - jnp.mean(values, axis=-1, keepdims=True)
    inverse = lax.rsqrt(jnp.mean(centred * centred, axis=-1, keepdims=True) + EPSILON)
    normal_part = centred * inverse
    return (normal_part * gain + shift, normal_part, inverse)


def norm_backward(upstream, normal_part, inverse, gain):
    scaled = upstream * gain
    inner = (
        scaled
        - jnp.mean(scaled, axis=-1, keepdims=True)
        - normal_part * jnp.mean(scaled * normal_part, axis=-1, keepdims=True)
    )
    return (inverse * inner, jnp.sum(upstream * normal_part, axis=0), jnp.sum(upstream, axis=0))


def gelu_value(pre):
    return 0.5 * pre * (1.0 + lax.erf(pre * ROOT_HALF))


def gelu_slope(pre):
    return 0.5 * (1.0 + lax.erf(pre * ROOT_HALF)) + pre * INV_ROOT_TWO_PI * jnp.exp(
        -0.5 * pre * pre
    )


def dot(a, b):
    return jnp.dot(a, b, preferred_element_type=F32)


def dot_nt(a, b):
    return lax.dot_general(a, b, (((1,), (1,)), ((), ())), preferred_element_type=F32)


def dot_tn(a, b):
    return lax.dot_general(a, b, (((0,), (0,)), ((), ())), preferred_element_type=F32)


def spread_heads(rows, heads):
    wide = rows.astype(F32)
    lane_head = lax.broadcasted_iota(jnp.int32, wide.shape, 1) // HD
    parts = [jnp.where(lane_head == h, wide, 0.0) for h in range(heads)]
    return jnp.concatenate(parts, axis=0).astype(BF)


def own_blocks(across, heads):
    return jnp.concatenate(
        [across[h * HD : (h + 1) * HD, h * QB : (h + 1) * QB] for h in range(heads)], axis=0
    )


def fill_bias(bias_ref, key_ref, query_row, off):
    bias_ref[...] = jnp.where(key_ref[...] == query_row, 0.0, NEG_LARGE)
    eye = lax.broadcasted_iota(jnp.int32, (QB, QB), 0) == lax.broadcasted_iota(
        jnp.int32, (QB, QB), 1
    )
    bias_ref[pl.ds(off, QB), :] = jnp.where(eye, 0.0, bias_ref[pl.ds(off, QB), :])


def forward_kernel(heads, x_ref, key_ref, seg_ref, o_ref, lse_ref, vt_ref, bias_ref):
    width = heads * HD
    total_rows = x_ref.shape[0]
    vt_ref[...] = x_ref[:, 2 * width : 3 * width].astype(F32).T.astype(BF)

    def step(i, carry):
        off = pl.multiple_of(i * QB, QB)
        query = spread_heads(x_ref[pl.ds(off, QB), 0:width] * (HD**-0.5), heads)
        fill_bias(bias_ref, key_ref, seg_ref[i], off)
        scores = dot_nt(x_ref[:, width : 2 * width], query)
        bias = bias_ref[...]
        scores = scores + jnp.concatenate([bias] * heads, axis=1)
        top = jnp.max(scores, axis=0, keepdims=True)
        expo = jnp.exp(scores - top)
        total = jnp.sum(expo, axis=0, keepdims=True)
        weights = (expo * (1.0 / total)).astype(BF)
        mixed = own_blocks(dot(vt_ref[...], weights), heads)
        o_ref[pl.ds(off, QB), :] = mixed.T.astype(BF)
        lse_ref[i] = top + jnp.log(total)
        return carry

    lax.fori_loop(0, total_rows // QB, step, 0)


def backward_kernel(
    heads,
    x_ref,
    o_ref,
    g_ref,
    lse_ref,
    key_ref,
    seg_ref,
    dx_ref,
    sums_ref,
    kt_ref,
    dk_ref,
    dv_ref,
    bias_ref,
):
    width = heads * HD
    total_rows = x_ref.shape[0]
    kt_ref[...] = x_ref[:, width : 2 * width].astype(F32).T.astype(BF)
    dk_ref[...] = jnp.zeros_like(dk_ref)
    dv_ref[...] = jnp.zeros_like(dv_ref)

    def step(i, query_sum):
        off = pl.multiple_of(i * QB, QB)
        query = spread_heads(x_ref[pl.ds(off, QB), 0:width] * (HD**-0.5), heads)
        g_rows = g_ref[pl.ds(off, QB), :]
        grad = spread_heads(g_rows, heads)
        product = (g_rows.astype(F32) * o_ref[pl.ds(off, QB), :].astype(F32)).T
        delta = jnp.concatenate(
            [
                jnp.sum(product[h * HD : (h + 1) * HD], axis=0, keepdims=True)
                for h in range(heads)
            ],
            axis=1,
        )
        fill_bias(bias_ref, key_ref, seg_ref[i], off)
        scores = dot_nt(x_ref[:, width : 2 * width], query)
        bias = bias_ref[...]
        probs = jnp.exp(scores + jnp.concatenate([bias] * heads, axis=1) - lse_ref[i])
        d_probs = dot_nt(x_ref[:, 2 * width : 3 * width], grad)
        dv_ref[...] += dot(probs.astype(BF), grad)
        d_scores = (probs * (d_probs - delta)).astype(BF)
        dk_ref[...] += dot(d_scores, query)
        d_query = own_blocks(dot(kt_ref[...], d_scores), heads).T * (HD**-0.5)
        dx_ref[pl.ds(off, QB), 0:width] = d_query.astype(BF)
        return query_sum + jnp.sum(d_query, axis=0, keepdims=True)

    query_sum = lax.fori_loop(0, total_rows // QB, step, jnp.zeros((1, width), F32))
    dx_ref[:, width : 2 * width] = dk_ref[...].astype(BF)
    dx_ref[:, 2 * width : 3 * width] = dv_ref[...].astype(BF)
    sums_ref[...] = jnp.concatenate(
        [query_sum, jnp.sum(dv_ref[...], axis=0, keepdims=True)], axis=0
    )


def attend_forward(x, key_codes, seg_rows, heads):
    rows = x.shape[0]
    width = heads * HD
    return pl.pallas_call(
        functools.partial(forward_kernel, heads),
        out_shape=(
            jax.ShapeDtypeStruct((rows, width), BF),
            jax.ShapeDtypeStruct((rows // QB, 1, heads * QB), F32),
        ),
        scratch_shapes=[pltpu.VMEM((width, rows), BF), pltpu.VMEM((rows, QB), F32)],
        cost_estimate=pl.CostEstimate(
            flops=4 * rows * rows * width,
            transcendentals=rows * rows * heads,
            bytes_accessed=rows * width * 8,
        ),
        name="attend_forward",
    )(x, key_codes, seg_rows)


def attend_backward(x, mixed, grad, lse, key_codes, seg_rows, heads):
    rows = x.shape[0]
    width = heads * HD
    return pl.pallas_call(
        functools.partial(backward_kernel, heads),
        out_shape=(
            jax.ShapeDtypeStruct((rows, 3 * width), BF),
            jax.ShapeDtypeStruct((2, width), F32),
        ),
        scratch_shapes=[
            pltpu.VMEM((width, rows), BF),
            pltpu.VMEM((rows, width), F32),
            pltpu.VMEM((rows, width), F32),
            pltpu.VMEM((rows, QB), F32),
        ],
        cost_estimate=pl.CostEstimate(
            flops=10 * rows * rows * width,
            transcendentals=rows * rows * heads,
            bytes_accessed=rows * width * 20,
        ),
        name="attend_backward",
    )(x, mixed, grad, lse, key_codes, seg_rows)


def after(value, *others):
    return lax.optimization_barrier((value, *others))[0]


def local(
    n,
    reps,
    tokens,
    segment_ids,
    valid_keys,
    norm_gain,
    norm_bias,
    qkv_weight,
    qv_bias,
    out_weight,
    up_weight,
    up_bias,
    down_weight,
    out_bias,
    layer_scale,
    cotangent,
):
    rows, width = tokens.shape
    ys = reps // 2
    local_heads = qv_bias.shape[2]
    hidden = up_weight.shape[2]
    heads = local_heads // n
    head_cols = heads * HD
    unit_cols = hidden // reps
    part = width // n
    z = lax.axis_index("fsdp")
    rep = lax.axis_index("rep")
    y, core = rep // 2, rep % 2
    first_tp = lax.axis_index("tp") == 0

    def z_pull(x, s):
        return lax.ppermute(x, "fsdp", [((j + s) % n, j) for j in range(n)])

    def z_push(x, s):
        return z_pull(x, n - s)

    def y_pull(x, d):
        return lax.ppermute(
            x, "rep", [(((a + d) % ys) * 2 + c, a * 2 + c) for a in range(ys) for c in range(2)]
        )

    def y_push(x, d):
        return y_pull(x, ys - d)

    def core_swap(x):
        return lax.ppermute(x, "rep", [(r, r ^ 1) for r in range(reps)])

    def gather_z(x):
        return [x] + [z_pull(x, s) for s in range(1, n)]

    def gather_rep(x):
        near = [x] + [y_pull(x, d) for d in range(1, ys)]
        return near + [core_swap(v) for v in near]

    slot_rep = [((y + d) % ys) * 2 + core for d in range(ys)]
    slot_rep = slot_rep + [((y + d) % ys) * 2 + 1 - core for d in range(ys)]

    def in_rep_order(slots, axis):
        stacked = jnp.stack(slots)
        picks = []
        for a in range(reps):
            slot = (a // 2 - y) % ys + ys * ((a % 2) ^ core)
            picks.append(lax.dynamic_index_in_dim(stacked, slot, 0, keepdims=False))
        return jnp.concatenate(picks, axis=axis)

    def from_own(x, axis, block):
        return lax.dynamic_slice_in_dim(
            jnp.concatenate([x, x], axis=axis), z * block, x.shape[axis], axis
        )

    def to_plain(x, axis, block):
        return lax.dynamic_slice_in_dim(
            jnp.concatenate([x, x], axis=axis), ((n - z) % n) * block, x.shape[axis], axis
        )

    def tp_swap(x):
        return lax.ppermute(x, "tp", [(0, 1), (1, 0)])

    def both_tp(x, other):
        return jnp.where(first_tp, x, other), jnp.where(first_tp, other, x)

    def exchange_heads(slots):
        stacked = jnp.stack(slots)
        outs = [
            lax.dynamic_index_in_dim(stacked, (z + n - s) % n, 0, keepdims=False)
            for s in range(n)
        ]
        blocks = [outs[0]] + [z_pull(outs[s], s) for s in range(1, n)]
        return jnp.concatenate(blocks, axis=0)

    def return_heads(x):
        blocks = [x[s * rows : (s + 1) * rows] for s in range(n)]
        return [blocks[0]] + [z_pull(blocks[n - s], s) for s in range(1, n)]

    q_cols = local_heads * HD // reps
    piece_qkv = lax.dynamic_slice_in_dim(qkv_weight[0], rep * q_cols, q_cols, 2).reshape(
        part, 3 * q_cols
    )
    gathered_qkv = gather_z(piece_qkv)

    codes = (segment_ids * 2 + valid_keys).astype(F32).astype(BF)
    code_rows = -(-rows // part)
    codes = jnp.pad(codes, (0, code_rows * part - rows)).reshape(code_rows, part)
    units = jnp.concatenate([qv_bias.reshape(2 * local_heads, -1), up_bias[0]])
    unit_shape = units.shape
    features = jnp.concatenate(
        [norm_gain[0], norm_bias[0], out_bias[0], layer_scale[0], codes, units.reshape(-1, part)]
    )
    gathered_features = gather_z(after(features, piece_qkv))

    piece_up = jnp.concatenate(
        [
            lax.dynamic_slice_in_dim(up_weight[0], rep * unit_cols, unit_cols, 1),
            lax.dynamic_slice_in_dim(out_weight[0], rep * q_cols, q_cols, 0).T,
        ],
        axis=1,
    )
    piece_down = lax.dynamic_slice_in_dim(down_weight[0], rep * unit_cols, unit_cols, 0)
    slots_qkv = gather_rep(jnp.concatenate(gathered_qkv, axis=0))
    gathered_up = gather_z(after(piece_up, *gathered_qkv))

    small = jnp.concatenate([f[:8] for f in gathered_features], axis=1).astype(F32)
    gains, shifts, biases, scales = small[0:2], small[2:4], small[4:6], small[6:8]
    all_codes = jnp.concatenate(
        [f[8 : 8 + code_rows].reshape(-1)[:rows] for f in gathered_features]
    )
    all_codes = all_codes.astype(jnp.int32)
    group_seg = all_codes // 2
    key_codes = jnp.where(all_codes % 2 == 1, group_seg, -1)
    group_rows = all_codes.shape[0]
    key_codes = jnp.broadcast_to(key_codes[:, None], (group_rows, QB))
    seg_rows = group_seg.reshape(group_rows // QB, 1, QB)
    unit_lanes = unit_shape[1]
    gathered_units = [f[8 + code_rows :].reshape(unit_shape) for f in gathered_features]
    units_full = to_plain(jnp.concatenate(gathered_units, axis=1), 1, unit_lanes).astype(F32)
    qv_full = units_full[: 2 * local_heads].reshape(2, local_heads * HD)
    up_full = units_full[2 * local_heads :].reshape(-1)
    qv_slots = [lax.dynamic_slice_in_dim(qv_full, r * q_cols, q_cols, 1) for r in slot_rep]
    up_slots = jnp.concatenate(
        [lax.dynamic_slice_in_dim(up_full, r * unit_cols, unit_cols, 0) for r in slot_rep]
    )
    bias_qkv = [jnp.concatenate([b[0], jnp.zeros((q_cols,), F32), b[1]]) for b in qv_slots]

    resid = from_own(tokens, 1, part).astype(F32)
    upstream = from_own(cotangent, 1, part).astype(F32)

    normed, part_one, inv_one = norm_forward(resid, gains[0], shifts[0])
    first_in = after(normed.astype(BF), key_codes, seg_rows)
    project = [(dot(first_in, w) + b).astype(BF) for w, b in zip(slots_qkv, bias_qkv)]
    x_heads = exchange_heads(project)
    quarter_up = jnp.concatenate(gathered_up, axis=0)
    quarter_out = quarter_up[:, unit_cols:]
    out_halves = both_tp(quarter_out, tp_swap(quarter_out))
    slots_up = gather_rep(jnp.concatenate([quarter_up[:, :unit_cols], *out_halves], axis=1))
    gathered_down = gather_z(after(piece_down, x_heads))
    mixed, lse = attend_forward(x_heads, key_codes, seg_rows, heads)
    mixed_back = return_heads(mixed)
    slots_down = gather_rep(jnp.concatenate(gathered_down, axis=1))
    mixed_flat = jnp.concatenate(
        [lax.select_n((k + n - z) % n, *mixed_back) for k in range(n)], axis=1
    )
    mixed_halves = both_tp(mixed_flat, tp_swap(mixed_flat))
    mixed_full = jnp.concatenate(
        [m[:, k * q_cols : (k + 1) * q_cols] for k in range(reps) for m in mixed_halves],
        axis=1,
    )
    w_out_full = jnp.concatenate([w[:, unit_cols:] for w in slots_up], axis=1)
    w_out = jnp.concatenate(
        [
            jnp.where(first_tp, w[:, unit_cols : unit_cols + q_cols], w[:, unit_cols + q_cols :])
            for w in slots_up
        ],
        axis=1,
    )
    w_up = jnp.concatenate([w[:, :unit_cols] for w in slots_up], axis=1)
    branch_one = dot_nt(mixed_full, w_out_full) + biases[0]
    resid_one = resid + scales[0] * branch_one
    normed_two, part_two, inv_two = norm_forward(resid_one, gains[1], shifts[1])
    second_in = normed_two.astype(BF)
    hidden_pre = dot(second_in, w_up) + up_slots
    hidden_act = gelu_value(hidden_pre).astype(BF)

    def sum_rep(lead, tail, slot_axis, sent=BF):
        total = lead + core_swap(tail)
        step = total.shape[slot_axis] // ys
        cuts = [lax.slice_in_dim(total, d * step, (d + 1) * step, axis=slot_axis) for d in range(ys)]
        mine = cuts[0]
        for d in range(1, ys):
            moved = y_push(cuts[d].astype(sent), d)
            mine = mine + moved.astype(F32)
        return mine

    def scatter_z(mine, z_axis, sent=F32):
        block = mine.shape[z_axis] // n
        wire = mine.astype(sent)
        result = lax.slice_in_dim(mine, 0, block, axis=z_axis)
        for s in range(1, n):
            cut = lax.slice_in_dim(wire, s * block, (s + 1) * block, axis=z_axis)
            moved = z_push(cut, s)
            result = result + moved.astype(F32)
        return gather_rep(result)

    branch_grad = (upstream * scales[1]).astype(BF)
    d_hidden = [
        dot_nt(branch_grad, w) * gelu_slope(hidden_pre[:, k * unit_cols : (k + 1) * unit_cols])
        for k, w in enumerate(slots_down)
    ]
    d_hidden_half = jnp.concatenate([v.astype(BF) for v in d_hidden], axis=1)
    partial_second = dot_nt(d_hidden_half, w_up)
    d_second = partial_second + tp_swap(partial_second)

    half = hidden // 2
    down_far = dot_tn(hidden_act[:, half:], branch_grad)
    up_far = dot_tn(second_in, d_hidden_half[:, half:])
    down_near = dot_tn(hidden_act[:, :half], branch_grad)
    up_near = dot_tn(second_in, d_hidden_half[:, :half])
    own_down = sum_rep(down_near, down_far, 0, F32)
    own_up = sum_rep(up_near, up_far, 1, F32)

    late_act = after(hidden_act, partial_second)
    partial_two = functools.reduce(
        jnp.add,
        [
            dot(late_act[:, k * unit_cols : (k + 1) * unit_cols], w)
            for k, w in enumerate(slots_down)
        ],
    )
    other_two = tp_swap(partial_two)
    d_norm_two = norm_backward(d_second, part_two, inv_two, gains[1])[0]
    upstream_one = upstream + d_norm_two
    branch_grad_one = (upstream_one * scales[0]).astype(BF)
    d_mixed = dot(branch_grad_one, w_out).astype(BF)
    g_heads = exchange_heads([d_mixed[:, k * head_cols : (k + 1) * head_cols] for k in range(n)])
    half = mixed_flat.shape[1] // 2
    out_far = dot_tn(mixed_flat[:, half:], branch_grad_one)
    out_near = dot_tn(mixed_flat[:, :half], branch_grad_one)
    own_out = sum_rep(out_near, out_far, 0)
    grad_down = scatter_z(own_down, 1, BF)
    dx_heads, head_sums = attend_backward(x_heads, mixed, g_heads, lse, key_codes, seg_rows, heads)
    dx_back = return_heads(dx_heads)

    late = lax.optimization_barrier(
        (
            upstream,
            upstream_one,
            branch_one,
            resid_one,
            partial_two,
            other_two,
            d_second,
            part_two,
            *d_hidden,
            dx_heads,
        )
    )
    late_up, late_up_one, late_one, late_resid, late_two, late_other, late_second, late_part = late[:8]
    late_hidden = late[8:-1]
    branch_two = late_two + late_other + biases[1]
    block_out = to_plain((late_resid + scales[1] * branch_two).astype(BF), 1, part)
    scale_two = jnp.sum(late_up * branch_two, axis=0)
    bias_two = jnp.sum(late_up, axis=0) * scales[1]
    scale_one = jnp.sum(late_up_one * late_one, axis=0)
    bias_one = jnp.sum(late_up_one, axis=0) * scales[0]
    gain_two = jnp.sum(late_second * late_part, axis=0)
    shift_two = jnp.sum(late_second, axis=0)

    grad_up = scatter_z(own_up, 0, BF)
    grad_out = scatter_z(own_out, 1, BF)
    cut = 2 * head_cols
    d_pair = jnp.concatenate(
        [lax.select_n((k + n - z) % n, *[v[:, :cut] for v in dx_back]) for k in range(n)], axis=1
    )
    d_value = jnp.concatenate(
        [lax.select_n((k + n - z) % n, *[v[:, cut:] for v in dx_back]) for k in range(n)], axis=1
    )
    half_v, half_p = d_value.shape[1] // 2, d_pair.shape[1] // 2
    value_far = dot_tn(first_in, d_value[:, half_v:])
    pair_far = dot_tn(first_in, d_pair[:, half_p:])
    value_near = dot_tn(first_in, d_value[:, :half_v])
    pair_near = dot_tn(first_in, d_pair[:, :half_p])
    own_value = sum_rep(value_near, value_far, 1)
    own_pair = sum_rep(pair_near, pair_far, 1)
    grad_value = scatter_z(own_value, 0)
    grad_pair = scatter_z(own_pair, 0)
    w_pair = jnp.concatenate([w[:, :cut] for w in slots_qkv], axis=1)
    w_value = jnp.concatenate([w[:, cut:] for w in slots_qkv], axis=1)
    partial_first = dot_nt(
        jnp.concatenate([d_pair, d_value], axis=1), jnp.concatenate([w_pair, w_value], axis=1)
    )
    d_first = partial_first + tp_swap(partial_first)
    d_norm_one, gain_one, shift_one = norm_backward(d_first, part_one, inv_one, gains[0])
    tokens_grad = to_plain(upstream_one + d_norm_one, 1, part)

    feature_grads = to_plain(
        jnp.stack(
            [gain_one, gain_two, shift_one, shift_two, bias_one, bias_two, scale_one, scale_two]
        ),
        1,
        part,
    )
    d_up_bias = [jnp.sum(after(v, own_pair), axis=0) for v in late_hidden]
    own_rep = lax.dynamic_index_in_dim(jnp.stack(slot_rep), z, 0, keepdims=False)
    qv_grads = lax.dynamic_update_slice_in_dim(
        jnp.zeros((2, local_heads * HD), F32), head_sums, own_rep * head_cols, 1
    )
    up_grads = in_rep_order(d_up_bias, 0)
    packed = jnp.concatenate(
        [feature_grads.reshape(-1), qv_grads.reshape(-1), up_grads]
    ).reshape(-1, 128)

    def total_over(values, position, count):
        stacked = jnp.stack(values)
        turned = lax.dynamic_slice_in_dim(
            jnp.concatenate([stacked, stacked]), (count - position) % count, count, 0
        )
        return jnp.sum(turned, axis=0)

    packed = total_over([packed] + [z_pull(packed, s) for s in range(1, n)], z, n)
    packed = total_over([packed] + [y_pull(packed, d) for d in range(1, ys)], y, ys)
    packed = packed + core_swap(packed)
    packed = packed.reshape(-1)
    size_f, size_q = 8 * width, 2 * local_heads * HD
    feature_grads = lax.dynamic_slice_in_dim(
        packed[:size_f].reshape(4, 2, width), z * part, part, 2
    )
    qv_grads = lax.dynamic_slice_in_dim(
        packed[size_f : size_f + size_q].reshape(2, local_heads, HD), z * unit_lanes, unit_lanes, 2
    )
    up_grads = lax.dynamic_slice_in_dim(
        packed[size_f + size_q :].reshape(-1, HD), z * unit_lanes, unit_lanes, 1
    )

    d_out, d_up = in_rep_order(grad_out, 0), in_rep_order(grad_up, 1)
    d_down = in_rep_order(grad_down, 0)
    d_qkv = jnp.concatenate(
        [
            in_rep_order([g.reshape(part, 2, q_cols) for g in grad_pair], 2),
            in_rep_order([g.reshape(part, 1, q_cols) for g in grad_value], 2),
        ],
        axis=1,
    )
    return (
        block_out,
        tokens_grad,
        feature_grads[0][None],
        feature_grads[1][None],
        d_qkv[None],
        qv_grads[None],
        d_out[None],
        d_up[None],
        up_grads[None],
        d_down[None],
        feature_grads[2][None],
        feature_grads[3][None],
    )


def solution(mesh):
    n, reps, tp = mesh.shape["fsdp"], mesh.shape["rep"], mesh.shape["tp"]
    assert n == reps and tp == 2
    by_token = P(("rep", "fsdp"), None)
    by_feature = P(None, None, "fsdp")
    by_row = P(None, "fsdp", "tp")
    by_column = P(None, "tp", "fsdp")
    placed = (
        by_token,
        P(("rep", "fsdp")),
        P(("rep", "fsdp")),
        by_feature,
        by_feature,
        P(None, "fsdp", None, "tp"),
        P(None, None, "tp", "fsdp"),
        by_column,
        by_row,
        by_column,
        by_column,
        by_feature,
        by_feature,
        by_token,
    )
    return jax.shard_map(
        functools.partial(local, n, reps),
        mesh=mesh,
        in_specs=placed,
        out_specs=(
            by_token,
            by_token,
            by_feature,
            by_feature,
            P(None, "fsdp", None, "tp"),
            P(None, None, "tp", "fsdp"),
            by_column,
            by_row,
            by_column,
            by_column,
            by_feature,
            by_feature,
        ),
        check_vma=False,
    )
```

```python
import functools

import jax
import jax.numpy as jnp
from jax import lax
from jax.experimental import pallas as pl
from jax.experimental.pallas import tpu as pltpu
from jax.sharding import PartitionSpec as P


HD = 64
QB = 128
EPSILON = 1e-06
ROOT_HALF = 0.7071067811865476
INV_ROOT_TWO_PI = 0.3989422804014327
NEG_LARGE = -1e30
BF = jnp.bfloat16
F32 = jnp.float32


def norm_forward(values, gain, shift):
    centred = values - jnp.mean(values, axis=-1, keepdims=True)
    inverse = lax.rsqrt(jnp.mean(centred * centred, axis=-1, keepdims=True) + EPSILON)
    normal_part = centred * inverse
    return (normal_part * gain + shift, normal_part, inverse)


def norm_backward(upstream, normal_part, inverse, gain):
    scaled = upstream * gain
    inner = (
        scaled
        - jnp.mean(scaled, axis=-1, keepdims=True)
        - normal_part * jnp.mean(scaled * normal_part, axis=-1, keepdims=True)
    )
    return (inverse * inner, jnp.sum(upstream * normal_part, axis=0), jnp.sum(upstream, axis=0))


def gelu_value(pre):
    return 0.5 * pre * (1.0 + lax.erf(pre * ROOT_HALF))


def gelu_slope(pre):
    return 0.5 * (1.0 + lax.erf(pre * ROOT_HALF)) + pre * INV_ROOT_TWO_PI * jnp.exp(
        -0.5 * pre * pre
    )


def dot(a, b):
    return jnp.dot(a, b, preferred_element_type=F32)


def dot_nt(a, b):
    return lax.dot_general(a, b, (((1,), (1,)), ((), ())), preferred_element_type=F32)


def dot_tn(a, b):
    return lax.dot_general(a, b, (((0,), (0,)), ((), ())), preferred_element_type=F32)


def spread_heads(rows, heads):
    wide = rows.astype(F32)
    lane_head = lax.broadcasted_iota(jnp.int32, wide.shape, 1) // HD
    parts = [jnp.where(lane_head == h, wide, 0.0) for h in range(heads)]
    return jnp.concatenate(parts, axis=0).astype(BF)


def own_blocks(across, heads):
    return jnp.concatenate(
        [across[h * HD : (h + 1) * HD, h * QB : (h + 1) * QB] for h in range(heads)], axis=0
    )


def fill_bias(bias_ref, key_ref, query_row, off):
    bias_ref[...] = jnp.where(key_ref[...] == query_row, 0.0, NEG_LARGE)
    eye = lax.broadcasted_iota(jnp.int32, (QB, QB), 0) == lax.broadcasted_iota(
        jnp.int32, (QB, QB), 1
    )
    bias_ref[pl.ds(off, QB), :] = jnp.where(eye, 0.0, bias_ref[pl.ds(off, QB), :])


def forward_kernel(heads, x_ref, key_ref, seg_ref, o_ref, lse_ref, vt_ref, bias_ref):
    width = heads * HD
    total_rows = x_ref.shape[0]
    vt_ref[...] = x_ref[:, 2 * width : 3 * width].astype(F32).T.astype(BF)

    def step(i, carry):
        off = pl.multiple_of(i * QB, QB)
        query = spread_heads(x_ref[pl.ds(off, QB), 0:width] * (HD**-0.5), heads)
        fill_bias(bias_ref, key_ref, seg_ref[i], off)
        scores = dot_nt(x_ref[:, width : 2 * width], query)
        bias = bias_ref[...]
        scores = scores + jnp.concatenate([bias] * heads, axis=1)
        top = jnp.max(scores, axis=0, keepdims=True)
        expo = jnp.exp(scores - top)
        total = jnp.sum(expo, axis=0, keepdims=True)
        weights = (expo * (1.0 / total)).astype(BF)
        mixed = own_blocks(dot(vt_ref[...], weights), heads)
        o_ref[pl.ds(off, QB), :] = mixed.T.astype(BF)
        lse_ref[i] = top + jnp.log(total)
        return carry

    lax.fori_loop(0, total_rows // QB, step, 0)


def backward_kernel(
    heads,
    x_ref,
    o_ref,
    g_ref,
    lse_ref,
    key_ref,
    seg_ref,
    dx_ref,
    sums_ref,
    kt_ref,
    dk_ref,
    dv_ref,
    bias_ref,
):
    width = heads * HD
    total_rows = x_ref.shape[0]
    kt_ref[...] = x_ref[:, width : 2 * width].astype(F32).T.astype(BF)
    dk_ref[...] = jnp.zeros_like(dk_ref)
    dv_ref[...] = jnp.zeros_like(dv_ref)

    def step(i, query_sum):
        off = pl.multiple_of(i * QB, QB)
        query = spread_heads(x_ref[pl.ds(off, QB), 0:width] * (HD**-0.5), heads)
        g_rows = g_ref[pl.ds(off, QB), :]
        grad = spread_heads(g_rows, heads)
        product = (g_rows.astype(F32) * o_ref[pl.ds(off, QB), :].astype(F32)).T
        delta = jnp.concatenate(
            [
                jnp.sum(product[h * HD : (h + 1) * HD], axis=0, keepdims=True)
                for h in range(heads)
            ],
            axis=1,
        )
        fill_bias(bias_ref, key_ref, seg_ref[i], off)
        scores = dot_nt(x_ref[:, width : 2 * width], query)
        bias = bias_ref[...]
        probs = jnp.exp(scores + jnp.concatenate([bias] * heads, axis=1) - lse_ref[i])
        d_probs = dot_nt(x_ref[:, 2 * width : 3 * width], grad)
        dv_ref[...] += dot(probs.astype(BF), grad)
        d_scores = (probs * (d_probs - delta)).astype(BF)
        dk_ref[...] += dot(d_scores, query)
        d_query = own_blocks(dot(kt_ref[...], d_scores), heads).T * (HD**-0.5)
        dx_ref[pl.ds(off, QB), 0:width] = d_query.astype(BF)
        return query_sum + jnp.sum(d_query, axis=0, keepdims=True)

    query_sum = lax.fori_loop(0, total_rows // QB, step, jnp.zeros((1, width), F32))
    dx_ref[:, width : 2 * width] = dk_ref[...].astype(BF)
    dx_ref[:, 2 * width : 3 * width] = dv_ref[...].astype(BF)
    sums_ref[...] = jnp.concatenate(
        [query_sum, jnp.sum(dv_ref[...], axis=0, keepdims=True)], axis=0
    )


def attend_forward(x, key_codes, seg_rows, heads):
    rows = x.shape[0]
    width = heads * HD
    return pl.pallas_call(
        functools.partial(forward_kernel, heads),
        out_shape=(
            jax.ShapeDtypeStruct((rows, width), BF),
            jax.ShapeDtypeStruct((rows // QB, 1, heads * QB), F32),
        ),
        scratch_shapes=[pltpu.VMEM((width, rows), BF), pltpu.VMEM((rows, QB), F32)],
        cost_estimate=pl.CostEstimate(
            flops=4 * rows * rows * width,
            transcendentals=rows * rows * heads,
            bytes_accessed=rows * width * 8,
        ),
        name="attend_forward",
    )(x, key_codes, seg_rows)


def attend_backward(x, mixed, grad, lse, key_codes, seg_rows, heads):
    rows = x.shape[0]
    width = heads * HD
    return pl.pallas_call(
        functools.partial(backward_kernel, heads),
        out_shape=(
            jax.ShapeDtypeStruct((rows, 3 * width), BF),
            jax.ShapeDtypeStruct((2, width), F32),
        ),
        scratch_shapes=[
            pltpu.VMEM((width, rows), BF),
            pltpu.VMEM((rows, width), F32),
            pltpu.VMEM((rows, width), F32),
            pltpu.VMEM((rows, QB), F32),
        ],
        cost_estimate=pl.CostEstimate(
            flops=10 * rows * rows * width,
            transcendentals=rows * rows * heads,
            bytes_accessed=rows * width * 20,
        ),
        name="attend_backward",
    )(x, mixed, grad, lse, key_codes, seg_rows)


def after(value, *others):
    return lax.optimization_barrier((value, *others))[0]


def local(
    n,
    reps,
    tokens,
    segment_ids,
    valid_keys,
    norm_gain,
    norm_bias,
    qkv_weight,
    qv_bias,
    out_weight,
    up_weight,
    up_bias,
    down_weight,
    out_bias,
    layer_scale,
    cotangent,
):
    rows, width = tokens.shape
    ys = reps // 2
    local_heads = qv_bias.shape[2]
    hidden = up_weight.shape[2]
    heads = local_heads // n
    head_cols = heads * HD
    unit_cols = hidden // reps
    part = width // n
    z = lax.axis_index("fsdp")
    rep = lax.axis_index("rep")
    y, core = rep // 2, rep % 2
    first_tp = lax.axis_index("tp") == 0

    def z_pull(x, s):
        return lax.ppermute(x, "fsdp", [((j + s) % n, j) for j in range(n)])

    def z_push(x, s):
        return z_pull(x, n - s)

    def y_pull(x, d):
        return lax.ppermute(
            x, "rep", [(((a + d) % ys) * 2 + c, a * 2 + c) for a in range(ys) for c in range(2)]
        )

    def y_push(x, d):
        return y_pull(x, ys - d)

    def core_swap(x):
        return lax.ppermute(x, "rep", [(r, r ^ 1) for r in range(reps)])

    def gather_z(x):
        return [x] + [z_pull(x, s) for s in range(1, n)]

    def gather_rep(x):
        near = [x] + [y_pull(x, d) for d in range(1, ys)]
        return near + [core_swap(v) for v in near]

    slot_rep = [((y + d) % ys) * 2 + core for d in range(ys)]
    slot_rep = slot_rep + [((y + d) % ys) * 2 + 1 - core for d in range(ys)]

    def in_rep_order(slots, axis):
        stacked = jnp.stack(slots)
        picks = []
        for a in range(reps):
            slot = (a // 2 - y) % ys + ys * ((a % 2) ^ core)
            picks.append(lax.dynamic_index_in_dim(stacked, slot, 0, keepdims=False))
        return jnp.concatenate(picks, axis=axis)

    def from_own(x, axis, block):
        return lax.dynamic_slice_in_dim(
            jnp.concatenate([x, x], axis=axis), z * block, x.shape[axis], axis
        )

    def to_plain(x, axis, block):
        return lax.dynamic_slice_in_dim(
            jnp.concatenate([x, x], axis=axis), ((n - z) % n) * block, x.shape[axis], axis
        )

    def tp_swap(x):
        return lax.ppermute(x, "tp", [(0, 1), (1, 0)])

    def both_tp(x, other):
        return jnp.where(first_tp, x, other), jnp.where(first_tp, other, x)

    def exchange_heads(slots):
        stacked = jnp.stack(slots)
        outs = [
            lax.dynamic_index_in_dim(stacked, (z + n - s) % n, 0, keepdims=False)
            for s in range(n)
        ]
        blocks = [outs[0]] + [z_pull(outs[s], s) for s in range(1, n)]
        return jnp.concatenate(blocks, axis=0)

    def return_heads(x):
        blocks = [x[s * rows : (s + 1) * rows] for s in range(n)]
        return [blocks[0]] + [z_pull(blocks[n - s], s) for s in range(1, n)]

    q_cols = local_heads * HD // reps
    piece_qkv = lax.dynamic_slice_in_dim(qkv_weight[0], rep * q_cols, q_cols, 2).reshape(
        part, 3 * q_cols
    )
    gathered_qkv = gather_z(piece_qkv)

    codes = (segment_ids * 2 + valid_keys).astype(F32).astype(BF)
    code_rows = -(-rows // part)
    codes = jnp.pad(codes, (0, code_rows * part - rows)).reshape(code_rows, part)
    units = jnp.concatenate([qv_bias.reshape(2 * local_heads, -1), up_bias[0]])
    unit_shape = units.shape
    features = jnp.concatenate(
        [norm_gain[0], norm_bias[0], out_bias[0], layer_scale[0], codes, units.reshape(-1, part)]
    )
    gathered_features = gather_z(after(features, piece_qkv))

    piece_up = jnp.concatenate(
        [
            lax.dynamic_slice_in_dim(up_weight[0], rep * unit_cols, unit_cols, 1),
            lax.dynamic_slice_in_dim(out_weight[0], rep * q_cols, q_cols, 0).T,
        ],
        axis=1,
    )
    piece_down = lax.dynamic_slice_in_dim(down_weight[0], rep * unit_cols, unit_cols, 0)
    slots_qkv = gather_rep(jnp.concatenate(gathered_qkv, axis=0))
    gathered_up = gather_z(after(piece_up, *gathered_qkv))

    small = jnp.concatenate([f[:8] for f in gathered_features], axis=1).astype(F32)
    gains, shifts, biases, scales = small[0:2], small[2:4], small[4:6], small[6:8]
    all_codes = jnp.concatenate(
        [f[8 : 8 + code_rows].reshape(-1)[:rows] for f in gathered_features]
    )
    all_codes = all_codes.astype(jnp.int32)
    group_seg = all_codes // 2
    key_codes = jnp.where(all_codes % 2 == 1, group_seg, -1)
    group_rows = all_codes.shape[0]
    key_codes = jnp.broadcast_to(key_codes[:, None], (group_rows, QB))
    seg_rows = group_seg.reshape(group_rows // QB, 1, QB)
    unit_lanes = unit_shape[1]
    gathered_units = [f[8 + code_rows :].reshape(unit_shape) for f in gathered_features]
    units_full = to_plain(jnp.concatenate(gathered_units, axis=1), 1, unit_lanes).astype(F32)
    qv_full = units_full[: 2 * local_heads].reshape(2, local_heads * HD)
    up_full = units_full[2 * local_heads :].reshape(-1)
    qv_slots = [lax.dynamic_slice_in_dim(qv_full, r * q_cols, q_cols, 1) for r in slot_rep]
    up_slots = jnp.concatenate(
        [lax.dynamic_slice_in_dim(up_full, r * unit_cols, unit_cols, 0) for r in slot_rep]
    )
    bias_qkv = [jnp.concatenate([b[0], jnp.zeros((q_cols,), F32), b[1]]) for b in qv_slots]

    resid = from_own(tokens, 1, part).astype(F32)
    upstream = from_own(cotangent, 1, part).astype(F32)

    normed, part_one, inv_one = norm_forward(resid, gains[0], shifts[0])
    first_in = after(normed.astype(BF), key_codes, seg_rows)
    project = [(dot(first_in, w) + b).astype(BF) for w, b in zip(slots_qkv, bias_qkv)]
    x_heads = exchange_heads(project)
    quarter_up = jnp.concatenate(gathered_up, axis=0)
    quarter_out = quarter_up[:, unit_cols:]
    out_halves = both_tp(quarter_out, tp_swap(quarter_out))
    slots_up = gather_rep(jnp.concatenate([quarter_up[:, :unit_cols], *out_halves], axis=1))
    gathered_down = gather_z(after(piece_down, x_heads))
    mixed, lse = attend_forward(x_heads, key_codes, seg_rows, heads)
    mixed_back = return_heads(mixed)
    slots_down = gather_rep(jnp.concatenate(gathered_down, axis=1))
    mixed_flat = jnp.concatenate(
        [lax.select_n((k + n - z) % n, *mixed_back) for k in range(n)], axis=1
    )
    mixed_halves = both_tp(mixed_flat, tp_swap(mixed_flat))
    mixed_full = jnp.concatenate(
        [m[:, k * q_cols : (k + 1) * q_cols] for k in range(reps) for m in mixed_halves],
        axis=1,
    )
    w_out_full = jnp.concatenate([w[:, unit_cols:] for w in slots_up], axis=1)
    w_out = jnp.concatenate(
        [
            jnp.where(first_tp, w[:, unit_cols : unit_cols + q_cols], w[:, unit_cols + q_cols :])
            for w in slots_up
        ],
        axis=1,
    )
    w_up = jnp.concatenate([w[:, :unit_cols] for w in slots_up], axis=1)
    branch_one = dot_nt(mixed_full, w_out_full) + biases[0]
    resid_one = resid + scales[0] * branch_one
    normed_two, part_two, inv_two = norm_forward(resid_one, gains[1], shifts[1])
    second_in = normed_two.astype(BF)
    hidden_pre = dot(second_in, w_up) + up_slots
    hidden_act = gelu_value(hidden_pre).astype(BF)

    def sum_rep(lead, tail, slot_axis, sent=BF):
        total = lead + core_swap(tail)
        step = total.shape[slot_axis] // ys
        cuts = [lax.slice_in_dim(total, d * step, (d + 1) * step, axis=slot_axis) for d in range(ys)]
        mine = cuts[0]
        for d in range(1, ys):
            moved = y_push(cuts[d].astype(sent), d)
            mine = mine + moved.astype(F32)
        return mine

    def scatter_z(mine, z_axis, sent=F32):
        block = mine.shape[z_axis] // n
        wire = mine.astype(sent)
        result = lax.slice_in_dim(mine, 0, block, axis=z_axis)
        for s in range(1, n):
            cut = lax.slice_in_dim(wire, s * block, (s + 1) * block, axis=z_axis)
            moved = z_push(cut, s)
            result = result + moved.astype(F32)
        return gather_rep(result)

    branch_grad = (upstream * scales[1]).astype(BF)
    d_hidden = [
        dot_nt(branch_grad, w) * gelu_slope(hidden_pre[:, k * unit_cols : (k + 1) * unit_cols])
        for k, w in enumerate(slots_down)
    ]
    d_hidden_half = jnp.concatenate([v.astype(BF) for v in d_hidden], axis=1)
    partial_second = dot_nt(d_hidden_half, w_up)
    d_second = partial_second + tp_swap(partial_second)

    half = hidden // 2
    down_far = dot_tn(hidden_act[:, half:], branch_grad)
    up_far = dot_tn(second_in, d_hidden_half[:, half:])
    down_near = dot_tn(hidden_act[:, :half], branch_grad)
    up_near = dot_tn(second_in, d_hidden_half[:, :half])
    own_down = sum_rep(down_near, down_far, 0, F32)
    own_up = sum_rep(up_near, up_far, 1, F32)

    late_act = after(hidden_act, partial_second)
    partial_two = functools.reduce(
        jnp.add,
        [
            dot(late_act[:, k * unit_cols : (k + 1) * unit_cols], w)
            for k, w in enumerate(slots_down)
        ],
    )
    other_two = tp_swap(partial_two)
    d_norm_two = norm_backward(d_second, part_two, inv_two, gains[1])[0]
    upstream_one = upstream + d_norm_two
    branch_grad_one = (upstream_one * scales[0]).astype(BF)
    d_mixed = dot(branch_grad_one, w_out).astype(BF)
    g_heads = exchange_heads([d_mixed[:, k * head_cols : (k + 1) * head_cols] for k in range(n)])
    half = mixed_flat.shape[1] // 2
    out_far = dot_tn(mixed_flat[:, half:], branch_grad_one)
    out_near = dot_tn(mixed_flat[:, :half], branch_grad_one)
    own_out = sum_rep(out_near, out_far, 0)
    grad_down = scatter_z(own_down, 1, BF)
    dx_heads, head_sums = attend_backward(x_heads, mixed, g_heads, lse, key_codes, seg_rows, heads)
    dx_back = return_heads(dx_heads)

    late = lax.optimization_barrier(
        (
            upstream,
            upstream_one,
            branch_one,
            resid_one,
            partial_two,
            other_two,
            d_second,
            part_two,
            *d_hidden,
            dx_heads,
        )
    )
    late_up, late_up_one, late_one, late_resid, late_two, late_other, late_second, late_part = late[:8]
    late_hidden = late[8:-1]
    branch_two = late_two + late_other + biases[1]
    block_out = to_plain((late_resid + scales[1] * branch_two).astype(BF), 1, part)
    scale_two = jnp.sum(late_up * branch_two, axis=0)
    bias_two = jnp.sum(late_up, axis=0) * scales[1]
    scale_one = jnp.sum(late_up_one * late_one, axis=0)
    bias_one = jnp.sum(late_up_one, axis=0) * scales[0]
    gain_two = jnp.sum(late_second * late_part, axis=0)
    shift_two = jnp.sum(late_second, axis=0)

    grad_up = scatter_z(own_up, 0, BF)
    grad_out = scatter_z(own_out, 1, BF)
    cut, slot_cols = 2 * head_cols, 3 * head_cols
    d_project = lax.optimization_barrier(
        jnp.concatenate([lax.select_n((k + n - z) % n, *dx_back) for k in range(n)], axis=1)
    )
    d_slots = [d_project[:, k * slot_cols : (k + 1) * slot_cols] for k in range(n)]
    near, far = d_slots[: n // 2], d_slots[n // 2 :]
    value_far = dot_tn(first_in, jnp.concatenate([v[:, cut:] for v in far], axis=1))
    pair_far = dot_tn(first_in, jnp.concatenate([v[:, :cut] for v in far], axis=1))
    value_near = dot_tn(first_in, jnp.concatenate([v[:, cut:] for v in near], axis=1))
    pair_near = dot_tn(first_in, jnp.concatenate([v[:, :cut] for v in near], axis=1))
    own_value = sum_rep(value_near, value_far, 1)
    own_pair = sum_rep(pair_near, pair_far, 1)
    grad_value = scatter_z(own_value, 0)
    grad_pair = scatter_z(own_pair, 0)
    w_qkv = jnp.concatenate(slots_qkv, axis=1)
    partial_first = dot_nt(d_project, w_qkv)
    d_first = partial_first + tp_swap(partial_first)
    d_norm_one, gain_one, shift_one = norm_backward(d_first, part_one, inv_one, gains[0])
    tokens_grad = to_plain(upstream_one + d_norm_one, 1, part)

    feature_grads = to_plain(
        jnp.stack(
            [gain_one, gain_two, shift_one, shift_two, bias_one, bias_two, scale_one, scale_two]
        ),
        1,
        part,
    )
    d_up_bias = [jnp.sum(after(v, own_pair), axis=0) for v in late_hidden]
    own_rep = lax.dynamic_index_in_dim(jnp.stack(slot_rep), z, 0, keepdims=False)
    qv_grads = lax.dynamic_update_slice_in_dim(
        jnp.zeros((2, local_heads * HD), F32), head_sums, own_rep * head_cols, 1
    )
    up_grads = in_rep_order(d_up_bias, 0)
    packed = jnp.concatenate(
        [feature_grads.reshape(-1), qv_grads.reshape(-1), up_grads]
    ).reshape(-1, 128)

    def total_over(values, position, count):
        stacked = jnp.stack(values)
        turned = lax.dynamic_slice_in_dim(
            jnp.concatenate([stacked, stacked]), (count - position) % count, count, 0
        )
        return jnp.sum(turned, axis=0)

    packed = total_over([packed] + [z_pull(packed, s) for s in range(1, n)], z, n)
    packed = total_over([packed] + [y_pull(packed, d) for d in range(1, ys)], y, ys)
    packed = packed + core_swap(packed)
    packed = packed.reshape(-1)
    size_f, size_q = 8 * width, 2 * local_heads * HD
    feature_grads = lax.dynamic_slice_in_dim(
        packed[:size_f].reshape(4, 2, width), z * part, part, 2
    )
    qv_grads = lax.dynamic_slice_in_dim(
        packed[size_f : size_f + size_q].reshape(2, local_heads, HD), z * unit_lanes, unit_lanes, 2
    )
    up_grads = lax.dynamic_slice_in_dim(
        packed[size_f + size_q :].reshape(-1, HD), z * unit_lanes, unit_lanes, 1
    )

    d_out, d_up = in_rep_order(grad_out, 0), in_rep_order(grad_up, 1)
    d_down = in_rep_order(grad_down, 0)
    d_qkv = jnp.concatenate(
        [
            in_rep_order([g.reshape(part, 2, q_cols) for g in grad_pair], 2),
            in_rep_order([g.reshape(part, 1, q_cols) for g in grad_value], 2),
        ],
        axis=1,
    )
    return (
        block_out,
        tokens_grad,
        feature_grads[0][None],
        feature_grads[1][None],
        d_qkv[None],
        qv_grads[None],
        d_out[None],
        d_up[None],
        up_grads[None],
        d_down[None],
        feature_grads[2][None],
        feature_grads[3][None],
    )


def solution(mesh):
    n, reps, tp = mesh.shape["fsdp"], mesh.shape["rep"], mesh.shape["tp"]
    assert n == reps and tp == 2
    by_token = P(("rep", "fsdp"), None)
    by_feature = P(None, None, "fsdp")
    by_row = P(None, "fsdp", "tp")
    by_column = P(None, "tp", "fsdp")
    placed = (
        by_token,
        P(("rep", "fsdp")),
        P(("rep", "fsdp")),
        by_feature,
        by_feature,
        P(None, "fsdp", None, "tp"),
        P(None, None, "tp", "fsdp"),
        by_column,
        by_row,
        by_column,
        by_column,
        by_feature,
        by_feature,
        by_token,
    )
    return jax.shard_map(
        functools.partial(local, n, reps),
        mesh=mesh,
        in_specs=placed,
        out_specs=(
            by_token,
            by_token,
            by_feature,
            by_feature,
            P(None, "fsdp", None, "tp"),
            P(None, None, "tp", "fsdp"),
            by_column,
            by_row,
            by_column,
            by_column,
            by_feature,
            by_feature,
        ),
        check_vma=False,
    )
```

```python
import functools

import jax
import jax.numpy as jnp
from jax import lax
from jax.experimental import pallas as pl
from jax.experimental.pallas import tpu as pltpu
from jax.sharding import PartitionSpec as P


HD = 64
QB = 128
EPSILON = 1e-06
ROOT_HALF = 0.7071067811865476
INV_ROOT_TWO_PI = 0.3989422804014327
NEG_LARGE = -1e30
BF = jnp.bfloat16
F32 = jnp.float32


def norm_forward(values, gain, shift):
    centred = values - jnp.mean(values, axis=-1, keepdims=True)
    inverse = lax.rsqrt(jnp.mean(centred * centred, axis=-1, keepdims=True) + EPSILON)
    normal_part = centred * inverse
    return (normal_part * gain + shift, normal_part, inverse)


def norm_backward(upstream, normal_part, inverse, gain):
    scaled = upstream * gain
    inner = (
        scaled
        - jnp.mean(scaled, axis=-1, keepdims=True)
        - normal_part * jnp.mean(scaled * normal_part, axis=-1, keepdims=True)
    )
    return (inverse * inner, jnp.sum(upstream * normal_part, axis=0), jnp.sum(upstream, axis=0))


def gelu_value(pre):
    return 0.5 * pre * (1.0 + lax.erf(pre * ROOT_HALF))


def gelu_slope(pre):
    return 0.5 * (1.0 + lax.erf(pre * ROOT_HALF)) + pre * INV_ROOT_TWO_PI * jnp.exp(
        -0.5 * pre * pre
    )


def dot(a, b):
    return jnp.dot(a, b, preferred_element_type=F32)


def dot_nt(a, b):
    return lax.dot_general(a, b, (((1,), (1,)), ((), ())), preferred_element_type=F32)


def dot_tn(a, b):
    return lax.dot_general(a, b, (((0,), (0,)), ((), ())), preferred_element_type=F32)


def spread_heads(rows, heads):
    wide = rows.astype(F32)
    lane_head = lax.broadcasted_iota(jnp.int32, wide.shape, 1) // HD
    parts = [jnp.where(lane_head == h, wide, 0.0) for h in range(heads)]
    return jnp.concatenate(parts, axis=0).astype(BF)


def own_blocks(across, heads):
    return jnp.concatenate(
        [across[h * HD : (h + 1) * HD, h * QB : (h + 1) * QB] for h in range(heads)], axis=0
    )


def fill_bias(bias_ref, key_ref, query_row, off):
    bias_ref[...] = jnp.where(key_ref[...] == query_row, 0.0, NEG_LARGE)
    eye = lax.broadcasted_iota(jnp.int32, (QB, QB), 0) == lax.broadcasted_iota(
        jnp.int32, (QB, QB), 1
    )
    bias_ref[pl.ds(off, QB), :] = jnp.where(eye, 0.0, bias_ref[pl.ds(off, QB), :])


def forward_kernel(heads, x_ref, key_ref, seg_ref, o_ref, lse_ref, vt_ref, bias_ref):
    width = heads * HD
    total_rows = x_ref.shape[0]
    vt_ref[...] = x_ref[:, 2 * width : 3 * width].astype(F32).T.astype(BF)

    def step(i, carry):
        off = pl.multiple_of(i * QB, QB)
        query = spread_heads(x_ref[pl.ds(off, QB), 0:width] * (HD**-0.5), heads)
        fill_bias(bias_ref, key_ref, seg_ref[i], off)
        scores = dot_nt(x_ref[:, width : 2 * width], query)
        bias = bias_ref[...]
        scores = scores + jnp.concatenate([bias] * heads, axis=1)
        top = jnp.max(scores, axis=0, keepdims=True)
        expo = jnp.exp(scores - top)
        total = jnp.sum(expo, axis=0, keepdims=True)
        weights = (expo * (1.0 / total)).astype(BF)
        mixed = own_blocks(dot(vt_ref[...], weights), heads)
        o_ref[pl.ds(off, QB), :] = mixed.T.astype(BF)
        lse_ref[i] = top + jnp.log(total)
        return carry

    lax.fori_loop(0, total_rows // QB, step, 0)


def backward_kernel(
    heads,
    x_ref,
    o_ref,
    g_ref,
    lse_ref,
    key_ref,
    seg_ref,
    dx_ref,
    sums_ref,
    kt_ref,
    dk_ref,
    dv_ref,
    bias_ref,
):
    width = heads * HD
    total_rows = x_ref.shape[0]
    kt_ref[...] = x_ref[:, width : 2 * width].astype(F32).T.astype(BF)
    dk_ref[...] = jnp.zeros_like(dk_ref)
    dv_ref[...] = jnp.zeros_like(dv_ref)

    def step(i, query_sum):
        off = pl.multiple_of(i * QB, QB)
        query = spread_heads(x_ref[pl.ds(off, QB), 0:width] * (HD**-0.5), heads)
        g_rows = g_ref[pl.ds(off, QB), :]
        grad = spread_heads(g_rows, heads)
        product = (g_rows.astype(F32) * o_ref[pl.ds(off, QB), :].astype(F32)).T
        delta = jnp.concatenate(
            [
                jnp.sum(product[h * HD : (h + 1) * HD], axis=0, keepdims=True)
                for h in range(heads)
            ],
            axis=1,
        )
        fill_bias(bias_ref, key_ref, seg_ref[i], off)
        scores = dot_nt(x_ref[:, width : 2 * width], query)
        bias = bias_ref[...]
        probs = jnp.exp(scores + jnp.concatenate([bias] * heads, axis=1) - lse_ref[i])
        d_probs = dot_nt(x_ref[:, 2 * width : 3 * width], grad)
        dv_ref[...] += dot(probs.astype(BF), grad)
        d_scores = (probs * (d_probs - delta)).astype(BF)
        dk_ref[...] += dot(d_scores, query)
        d_query = own_blocks(dot(kt_ref[...], d_scores), heads).T * (HD**-0.5)
        dx_ref[pl.ds(off, QB), 0:width] = d_query.astype(BF)
        return query_sum + jnp.sum(d_query, axis=0, keepdims=True)

    query_sum = lax.fori_loop(0, total_rows // QB, step, jnp.zeros((1, width), F32))
    dx_ref[:, width : 2 * width] = dk_ref[...].astype(BF)
    dx_ref[:, 2 * width : 3 * width] = dv_ref[...].astype(BF)
    sums_ref[...] = jnp.concatenate(
        [query_sum, jnp.sum(dv_ref[...], axis=0, keepdims=True)], axis=0
    )


def attend_forward(x, key_codes, seg_rows, heads):
    rows = x.shape[0]
    width = heads * HD
    return pl.pallas_call(
        functools.partial(forward_kernel, heads),
        out_shape=(
            jax.ShapeDtypeStruct((rows, width), BF),
            jax.ShapeDtypeStruct((rows // QB, 1, heads * QB), F32),
        ),
        scratch_shapes=[pltpu.VMEM((width, rows), BF), pltpu.VMEM((rows, QB), F32)],
        cost_estimate=pl.CostEstimate(
            flops=4 * rows * rows * width,
            transcendentals=rows * rows * heads,
            bytes_accessed=rows * width * 8,
        ),
        name="attend_forward",
    )(x, key_codes, seg_rows)


def attend_backward(x, mixed, grad, lse, key_codes, seg_rows, heads):
    rows = x.shape[0]
    width = heads * HD
    return pl.pallas_call(
        functools.partial(backward_kernel, heads),
        out_shape=(
            jax.ShapeDtypeStruct((rows, 3 * width), BF),
            jax.ShapeDtypeStruct((2, width), F32),
        ),
        scratch_shapes=[
            pltpu.VMEM((width, rows), BF),
            pltpu.VMEM((rows, width), F32),
            pltpu.VMEM((rows, width), F32),
            pltpu.VMEM((rows, QB), F32),
        ],
        cost_estimate=pl.CostEstimate(
            flops=10 * rows * rows * width,
            transcendentals=rows * rows * heads,
            bytes_accessed=rows * width * 20,
        ),
        name="attend_backward",
    )(x, mixed, grad, lse, key_codes, seg_rows)


def after(value, *others):
    return lax.optimization_barrier((value, *others))[0]


def local(
    n,
    reps,
    tokens,
    segment_ids,
    valid_keys,
    norm_gain,
    norm_bias,
    qkv_weight,
    qv_bias,
    out_weight,
    up_weight,
    up_bias,
    down_weight,
    out_bias,
    layer_scale,
    cotangent,
):
    rows, width = tokens.shape
    ys = reps // 2
    local_heads = qv_bias.shape[2]
    hidden = up_weight.shape[2]
    heads = local_heads // n
    head_cols = heads * HD
    unit_cols = hidden // reps
    part = width // n
    z = lax.axis_index("fsdp")
    rep = lax.axis_index("rep")
    y, core = rep // 2, rep % 2
    first_tp = lax.axis_index("tp") == 0

    def z_pull(x, s):
        return lax.ppermute(x, "fsdp", [((j + s) % n, j) for j in range(n)])

    def z_push(x, s):
        return z_pull(x, n - s)

    def y_pull(x, d):
        return lax.ppermute(
            x, "rep", [(((a + d) % ys) * 2 + c, a * 2 + c) for a in range(ys) for c in range(2)]
        )

    def y_push(x, d):
        return y_pull(x, ys - d)

    def core_swap(x):
        return lax.ppermute(x, "rep", [(r, r ^ 1) for r in range(reps)])

    def gather_z(x):
        return [x] + [z_pull(x, s) for s in range(1, n)]

    def gather_rep(x):
        near = [x] + [y_pull(x, d) for d in range(1, ys)]
        return near + [core_swap(v) for v in near]

    slot_rep = [((y + d) % ys) * 2 + core for d in range(ys)]
    slot_rep = slot_rep + [((y + d) % ys) * 2 + 1 - core for d in range(ys)]

    def in_rep_order(slots, axis):
        stacked = jnp.stack(slots)
        picks = []
        for a in range(reps):
            slot = (a // 2 - y) % ys + ys * ((a % 2) ^ core)
            picks.append(lax.dynamic_index_in_dim(stacked, slot, 0, keepdims=False))
        return jnp.concatenate(picks, axis=axis)

    def from_own(x, axis, block):
        return lax.dynamic_slice_in_dim(
            jnp.concatenate([x, x], axis=axis), z * block, x.shape[axis], axis
        )

    def to_plain(x, axis, block):
        return lax.dynamic_slice_in_dim(
            jnp.concatenate([x, x], axis=axis), ((n - z) % n) * block, x.shape[axis], axis
        )

    def tp_swap(x):
        return lax.ppermute(x, "tp", [(0, 1), (1, 0)])

    def both_tp(x, other):
        return jnp.where(first_tp, x, other), jnp.where(first_tp, other, x)

    def exchange_heads(slots):
        stacked = jnp.stack(slots)
        outs = [
            lax.dynamic_index_in_dim(stacked, (z + n - s) % n, 0, keepdims=False)
            for s in range(n)
        ]
        blocks = [outs[0]] + [z_pull(outs[s], s) for s in range(1, n)]
        return jnp.concatenate(blocks, axis=0)

    def return_heads(x):
        blocks = [x[s * rows : (s + 1) * rows] for s in range(n)]
        return [blocks[0]] + [z_pull(blocks[n - s], s) for s in range(1, n)]

    q_cols = local_heads * HD // reps
    piece_qkv = lax.dynamic_slice_in_dim(qkv_weight[0], rep * q_cols, q_cols, 2).reshape(
        part, 3 * q_cols
    )
    gathered_qkv = gather_z(piece_qkv)

    codes = (segment_ids * 2 + valid_keys).astype(F32).astype(BF)
    code_rows = -(-rows // part)
    codes = jnp.pad(codes, (0, code_rows * part - rows)).reshape(code_rows, part)
    units = jnp.concatenate([qv_bias.reshape(2 * local_heads, -1), up_bias[0]])
    unit_shape = units.shape
    features = jnp.concatenate(
        [norm_gain[0], norm_bias[0], out_bias[0], layer_scale[0], codes, units.reshape(-1, part)]
    )
    gathered_features = gather_z(after(features, piece_qkv))

    piece_up = jnp.concatenate(
        [
            lax.dynamic_slice_in_dim(up_weight[0], rep * unit_cols, unit_cols, 1),
            lax.dynamic_slice_in_dim(out_weight[0], rep * q_cols, q_cols, 0).T,
        ],
        axis=1,
    )
    piece_down = lax.dynamic_slice_in_dim(down_weight[0], rep * unit_cols, unit_cols, 0)
    slots_qkv = gather_rep(jnp.concatenate(gathered_qkv, axis=0))
    gathered_up = gather_z(after(piece_up, *gathered_qkv))

    small = jnp.concatenate([f[:8] for f in gathered_features], axis=1).astype(F32)
    gains, shifts, biases, scales = small[0:2], small[2:4], small[4:6], small[6:8]
    all_codes = jnp.concatenate(
        [f[8 : 8 + code_rows].reshape(-1)[:rows] for f in gathered_features]
    )
    all_codes = all_codes.astype(jnp.int32)
    group_seg = all_codes // 2
    key_codes = jnp.where(all_codes % 2 == 1, group_seg, -1)
    group_rows = all_codes.shape[0]
    key_codes = jnp.broadcast_to(key_codes[:, None], (group_rows, QB))
    seg_rows = group_seg.reshape(group_rows // QB, 1, QB)
    unit_lanes = unit_shape[1]
    gathered_units = [f[8 + code_rows :].reshape(unit_shape) for f in gathered_features]
    units_full = to_plain(jnp.concatenate(gathered_units, axis=1), 1, unit_lanes).astype(F32)
    qv_full = units_full[: 2 * local_heads].reshape(2, local_heads * HD)
    up_full = units_full[2 * local_heads :].reshape(-1)
    qv_slots = [lax.dynamic_slice_in_dim(qv_full, r * q_cols, q_cols, 1) for r in slot_rep]
    up_slots = jnp.concatenate(
        [lax.dynamic_slice_in_dim(up_full, r * unit_cols, unit_cols, 0) for r in slot_rep]
    )
    bias_qkv = [jnp.concatenate([b[0], jnp.zeros((q_cols,), F32), b[1]]) for b in qv_slots]

    resid = from_own(tokens, 1, part).astype(F32)
    upstream = from_own(cotangent, 1, part).astype(F32)

    normed, part_one, inv_one = norm_forward(resid, gains[0], shifts[0])
    first_in = after(normed.astype(BF), key_codes, seg_rows)
    project = [(dot(first_in, w) + b).astype(BF) for w, b in zip(slots_qkv, bias_qkv)]
    x_heads = exchange_heads(project)
    quarter_up = jnp.concatenate(gathered_up, axis=0)
    quarter_out = quarter_up[:, unit_cols:]
    out_halves = both_tp(quarter_out, tp_swap(quarter_out))
    slots_up = gather_rep(jnp.concatenate([quarter_up[:, :unit_cols], *out_halves], axis=1))
    gathered_down = gather_z(after(piece_down, x_heads))
    mixed, lse = attend_forward(x_heads, key_codes, seg_rows, heads)
    mixed_back = return_heads(mixed)
    slots_down = gather_rep(jnp.concatenate(gathered_down, axis=1))
    mixed_flat = jnp.concatenate(
        [lax.select_n((k + n - z) % n, *mixed_back) for k in range(n)], axis=1
    )
    mixed_halves = both_tp(mixed_flat, tp_swap(mixed_flat))
    mixed_full = jnp.concatenate(
        [m[:, k * q_cols : (k + 1) * q_cols] for k in range(reps) for m in mixed_halves],
        axis=1,
    )
    w_out_full = jnp.concatenate([w[:, unit_cols:] for w in slots_up], axis=1)
    w_out = jnp.concatenate(
        [
            jnp.where(first_tp, w[:, unit_cols : unit_cols + q_cols], w[:, unit_cols + q_cols :])
            for w in slots_up
        ],
        axis=1,
    )
    w_up = jnp.concatenate([w[:, :unit_cols] for w in slots_up], axis=1)
    branch_one = dot_nt(mixed_full, w_out_full) + biases[0]
    resid_one = resid + scales[0] * branch_one
    normed_two, part_two, inv_two = norm_forward(resid_one, gains[1], shifts[1])
    second_in = normed_two.astype(BF)
    hidden_pre = dot(second_in, w_up) + up_slots
    hidden_act = gelu_value(hidden_pre).astype(BF)

    def sum_rep(lead, tail, slot_axis, sent=BF):
        total = lead + core_swap(tail)
        step = total.shape[slot_axis] // ys
        cuts = [lax.slice_in_dim(total, d * step, (d + 1) * step, axis=slot_axis) for d in range(ys)]
        mine = cuts[0]
        for d in range(1, ys):
            moved = y_push(cuts[d].astype(sent), d)
            mine = mine + moved.astype(F32)
        return mine

    def scatter_z(mine, z_axis, sent=F32):
        block = mine.shape[z_axis] // n
        wire = mine.astype(sent)
        result = lax.slice_in_dim(mine, 0, block, axis=z_axis)
        for s in range(1, n):
            cut = lax.slice_in_dim(wire, s * block, (s + 1) * block, axis=z_axis)
            moved = z_push(cut, s)
            result = result + moved.astype(F32)
        return gather_rep(result)

    branch_grad = (upstream * scales[1]).astype(BF)
    d_hidden = [
        dot_nt(branch_grad, w) * gelu_slope(hidden_pre[:, k * unit_cols : (k + 1) * unit_cols])
        for k, w in enumerate(slots_down)
    ]
    d_hidden_half = jnp.concatenate([v.astype(BF) for v in d_hidden], axis=1)
    partial_second = dot_nt(d_hidden_half, w_up)
    d_second = partial_second + tp_swap(partial_second)

    half = hidden // 2
    down_far = dot_tn(hidden_act[:, half:], branch_grad)
    up_far = dot_tn(second_in, d_hidden_half[:, half:])
    down_near = dot_tn(hidden_act[:, :half], branch_grad)
    up_near = dot_tn(second_in, d_hidden_half[:, :half])
    own_down = sum_rep(down_near, down_far, 0, F32)
    own_up = sum_rep(up_near, up_far, 1, F32)

    late_act = after(hidden_act, partial_second)
    partial_two = functools.reduce(
        jnp.add,
        [
            dot(late_act[:, k * unit_cols : (k + 1) * unit_cols], w)
            for k, w in enumerate(slots_down)
        ],
    )
    other_two = tp_swap(partial_two)
    d_norm_two = norm_backward(d_second, part_two, inv_two, gains[1])[0]
    upstream_one = upstream + d_norm_two
    branch_grad_one = (upstream_one * scales[0]).astype(BF)
    d_mixed = dot(branch_grad_one, w_out).astype(BF)
    g_heads = exchange_heads([d_mixed[:, k * head_cols : (k + 1) * head_cols] for k in range(n)])
    half = mixed_flat.shape[1] // 2
    out_far = dot_tn(mixed_flat[:, half:], branch_grad_one)
    out_near = dot_tn(mixed_flat[:, :half], branch_grad_one)
    own_out = sum_rep(out_near, out_far, 0)
    grad_down = scatter_z(own_down, 1, BF)
    dx_heads, head_sums = attend_backward(x_heads, mixed, g_heads, lse, key_codes, seg_rows, heads)
    dx_back = return_heads(dx_heads)

    late = lax.optimization_barrier(
        (
            upstream,
            upstream_one,
            branch_one,
            resid_one,
            partial_two,
            other_two,
            d_second,
            part_two,
            *d_hidden,
            dx_heads,
        )
    )
    late_up, late_up_one, late_one, late_resid, late_two, late_other, late_second, late_part = late[:8]
    late_hidden = late[8:-1]
    branch_two = late_two + late_other + biases[1]
    block_out = to_plain((late_resid + scales[1] * branch_two).astype(BF), 1, part)
    scale_two = jnp.sum(late_up * branch_two, axis=0)
    bias_two = jnp.sum(late_up, axis=0) * scales[1]
    scale_one = jnp.sum(late_up_one * late_one, axis=0)
    bias_one = jnp.sum(late_up_one, axis=0) * scales[0]
    gain_two = jnp.sum(late_second * late_part, axis=0)
    shift_two = jnp.sum(late_second, axis=0)
    d_up_bias = [jnp.sum(v, axis=0) for v in late_hidden]

    grad_up = scatter_z(own_up, 0, BF)
    grad_out = scatter_z(own_out, 1, BF)
    d_project = jnp.concatenate(
        [lax.select_n((k + n - z) % n, *dx_back) for k in range(n)], axis=1
    )
    half = d_project.shape[1] // 2
    qkv_far = dot_tn(first_in, d_project[:, half:])
    qkv_near = dot_tn(first_in, d_project[:, :half])
    grad_qkv = scatter_z(sum_rep(qkv_near, qkv_far, 1), 0)
    w_qkv = jnp.concatenate(slots_qkv, axis=1)
    partial_first = dot_nt(d_project, w_qkv)
    d_first = partial_first + tp_swap(partial_first)
    d_norm_one, gain_one, shift_one = norm_backward(d_first, part_one, inv_one, gains[0])
    tokens_grad = to_plain(upstream_one + d_norm_one, 1, part)

    feature_grads = to_plain(
        jnp.stack(
            [gain_one, gain_two, shift_one, shift_two, bias_one, bias_two, scale_one, scale_two]
        ),
        1,
        part,
    )
    own_rep = lax.dynamic_index_in_dim(jnp.stack(slot_rep), z, 0, keepdims=False)
    qv_grads = lax.dynamic_update_slice_in_dim(
        jnp.zeros((2, local_heads * HD), F32), head_sums, own_rep * head_cols, 1
    )
    up_grads = in_rep_order(d_up_bias, 0)
    packed = jnp.concatenate(
        [feature_grads.reshape(-1), qv_grads.reshape(-1), up_grads]
    ).reshape(-1, 128)

    def total_over(values, position, count):
        stacked = jnp.stack(values)
        turned = lax.dynamic_slice_in_dim(
            jnp.concatenate([stacked, stacked]), (count - position) % count, count, 0
        )
        return jnp.sum(turned, axis=0)

    packed = total_over([packed] + [z_pull(packed, s) for s in range(1, n)], z, n)
    packed = total_over([packed] + [y_pull(packed, d) for d in range(1, ys)], y, ys)
    packed = packed + core_swap(packed)
    packed = packed.reshape(-1)
    size_f, size_q = 8 * width, 2 * local_heads * HD
    feature_grads = lax.dynamic_slice_in_dim(
        packed[:size_f].reshape(4, 2, width), z * part, part, 2
    )
    qv_grads = lax.dynamic_slice_in_dim(
        packed[size_f : size_f + size_q].reshape(2, local_heads, HD), z * unit_lanes, unit_lanes, 2
    )
    up_grads = lax.dynamic_slice_in_dim(
        packed[size_f + size_q :].reshape(-1, HD), z * unit_lanes, unit_lanes, 1
    )

    d_out, d_up = in_rep_order(grad_out, 0), in_rep_order(grad_up, 1)
    d_down = in_rep_order(grad_down, 0)
    d_qkv = in_rep_order([g.reshape(part, 3, q_cols) for g in grad_qkv], 2)
    return (
        block_out,
        tokens_grad,
        feature_grads[0][None],
        feature_grads[1][None],
        d_qkv[None],
        qv_grads[None],
        d_out[None],
        d_up[None],
        up_grads[None],
        d_down[None],
        feature_grads[2][None],
        feature_grads[3][None],
    )


def solution(mesh):
    n, reps, tp = mesh.shape["fsdp"], mesh.shape["rep"], mesh.shape["tp"]
    assert n == reps and tp == 2
    by_token = P(("rep", "fsdp"), None)
    by_feature = P(None, None, "fsdp")
    by_row = P(None, "fsdp", "tp")
    by_column = P(None, "tp", "fsdp")
    placed = (
        by_token,
        P(("rep", "fsdp")),
        P(("rep", "fsdp")),
        by_feature,
        by_feature,
        P(None, "fsdp", None, "tp"),
        P(None, None, "tp", "fsdp"),
        by_column,
        by_row,
        by_column,
        by_column,
        by_feature,
        by_feature,
        by_token,
    )
    return jax.shard_map(
        functools.partial(local, n, reps),
        mesh=mesh,
        in_specs=placed,
        out_specs=(
            by_token,
            by_token,
            by_feature,
            by_feature,
            P(None, "fsdp", None, "tp"),
            P(None, None, "tp", "fsdp"),
            by_column,
            by_row,
            by_column,
            by_column,
            by_feature,
            by_feature,
        ),
        check_vma=False,
    )
```
